128 devices in a mesh: seq: 16 (over z, y_hi, core), grp: 8 (over x, y_lo).
Axes of the slice: x: 4, y: 4 (y_hi: 2, y_lo: 2; y = y_hi * 2 + y_lo), z: 4, core: 2. Of those that a mesh axis runs over, the one named last changes fastest.
Arguments:
- tokens: bfloat16 [262144, 1280], P(('seq', 'grp')), may hold values from -27 to 27
- slot_keys: bfloat16 [1280, 512], replicated, may hold values from -1.5 to 1.5
- norm_gain: float32 [128, 1280], P(('seq', 'grp')), may hold values from 0.1 to 1.9
- w_in: bfloat16 [128, 1280, 2560], P(('seq', 'grp')), may hold values from -0.15625 to 0.15625
- w_out: bfloat16 [128, 2560, 1280], P(('seq', 'grp')), may hold values from -0.125 to 0.125
Outputs:
- mixed: bfloat16 [262144, 1280], P(('seq', 'grp'))
The draws below stay inside these ranges and needn't reach their ends.
All inputs are finite; a program needn't handle non-finite values.
Results may differ from the reference program's by a relative error of at most 0.007.
Values may be sent and summed in bfloat16 or wider, within the bound.
A program may use at most 128 MiB of HBM per device.

```python
import jax
import jax.numpy as jnp
from jax import lax

D = 1280
FF = 2560
SLOTS_PER = 4
TOK_DEV = 2048
EXPERTS = 128
SLOTS = 512
TOKENS = 262144


def slot_table(key):
    sub = jax.random.fold_in(key, 7)
    table = jax.random.normal(sub, (D, SLOTS), jnp.float32) * (3.0 / jnp.sqrt(jnp.float32(D)))
    return jnp.clip(table, -1.5, 1.5)


def draw_slot_keys(key, part):
    return slot_table(key).astype(jnp.bfloat16)


def draw_tokens(key, part):
    base = jnp.clip(jax.random.normal(jax.random.fold_in(key, 11), (TOKENS, D), jnp.float32), -6.0, 6.0)
    bound = 24.0 + 4000 // D
    return jnp.clip(base, -bound, bound).astype(jnp.bfloat16)


def level_of(stream_key, shape, cuts, low, top_value):
    factor_of = 1.0
    for position, parts in cuts:
        heights = jax.random.uniform(jax.random.fold_in(jax.random.fold_in(stream_key, 6), position), (parts,), jnp.float32, low / len(cuts), top_value / len(cuts))
        factor_of = factor_of * jnp.repeat(jnp.exp(heights), shape[position] // parts).reshape((-1,) + (1,) * (len(shape) - 1 - position))
    return factor_of


def centred(rng, shape, spread, most, shards=(), held_as=jnp.bfloat16):
    values = spread * jax.random.normal(rng, shape, jnp.float32)
    if shards:
        values = values * level_of(rng, shape, shards, -0.22, 0.18)
    return jnp.clip(values, -most, most).astype(held_as)


def setup_inputs(seed: int = 0) -> dict:
    key_of = jax.random.split(jax.random.key(seed), 6)
    return {
        "tokens": draw_tokens(jax.random.fold_in(key_of[5], 71), 0),
        "slot_keys": draw_slot_keys(jax.random.fold_in(key_of[5], 71), 0),
        "norm_gain": jnp.clip(1.0 + 0.18 * jax.random.normal(key_of[2], (EXPERTS, D), jnp.float32), 0.1, 1.9),
        "w_in": centred(key_of[3], (EXPERTS, D, FF), D ** -0.5, 0.15625, ((0, 128),)),
        "w_out": centred(key_of[4], (EXPERTS, FF, D), FF ** -0.5, 0.125, ((0, 128),)),
    }


def reference(tokens, slot_keys, norm_gain, w_in, w_out):
    blocks = tokens.reshape(TOKENS // TOK_DEV, TOK_DEV, D)

    def dispatch_step(carry, block):
        top, numer, total = carry
        logits = jnp.dot(block, slot_keys, preferred_element_type=jnp.float32)
        peak = jnp.max(logits, axis=0)
        scores = jnp.exp(logits - peak[None, :])
        weights = scores.astype(jnp.bfloat16)
        part = jnp.dot(weights.T, block, preferred_element_type=jnp.float32)
        newtop = jnp.maximum(top, peak)
        older = jnp.exp(top - newtop)
        newer = jnp.exp(peak - newtop)
        numer = numer * older[:, None] + part * newer[:, None]
        total = total * older + jnp.sum(scores, axis=0) * newer
        return (newtop, numer, total), None

    start = (jnp.full((SLOTS,), -jnp.inf, jnp.float32), jnp.zeros((SLOTS, D), jnp.float32), jnp.zeros((SLOTS,), jnp.float32))
    (top, numer, total), unused = lax.scan(dispatch_step, start, blocks)
    slot_in = (numer / total[:, None]).reshape(EXPERTS, SLOTS_PER, D)
    normed = (slot_in * norm_gain[:, None, :]).astype(jnp.bfloat16)

    def expert_step(items):
        rows, first, second = items
        hidden = jax.nn.gelu(jnp.dot(rows, first, preferred_element_type=jnp.float32)).astype(jnp.bfloat16)
        return jnp.dot(hidden, second, preferred_element_type=jnp.float32).astype(jnp.bfloat16)

    expert_out = lax.map(expert_step, (normed, w_in, w_out)).reshape(SLOTS, D)

    def combine_step(block):
        logits = jnp.dot(block, slot_keys, preferred_element_type=jnp.float32)
        row_top = jnp.max(logits, axis=1, keepdims=True)
        row_exp = jnp.exp(logits - row_top)
        combine = (row_exp / jnp.sum(row_exp, axis=1, keepdims=True)).astype(jnp.bfloat16)
        return jnp.dot(combine, expert_out, preferred_element_type=jnp.float32).astype(jnp.bfloat16)

    mixed = lax.map(combine_step, blocks)
    return mixed.reshape(TOKENS, D)
```

```python
import jax
import jax.numpy as jnp
from jax import lax
from jax.experimental import pallas as pl
from jax.experimental.pallas import tpu as pltpu
from jax.sharding import PartitionSpec as P

F32 = jnp.float32
BF16 = jnp.bfloat16
MESH = pl.DeviceIdType.MESH
TOK, D, FF, SLOTS = 2048, 1280, 2560, 512
TILE = 256
TILES = TOK // TILE
WIDE = 256
CHUNKS = D // WIDE
SPLIT = 512
ORDER = (2, 0, 3, 1, 4)
S_AUX0, S_AUXA, S_AUXB, S_AUXY = 0, 1, 7, 13
S_CORE = 16
S_ONE = 21
S_TWO = 36
S_Y = 42
S_GY = 45
S_G2 = 48
S_G3 = 54
S_GC = 60
N_SEM = 68


def place():
    seq = lax.axis_index("seq")
    grp = lax.axis_index("grp")
    return {"z": seq // 4, "yh": (seq // 2) % 2, "c": seq % 2, "x": grp // 2, "yl": grp % 2}


def device(at):
    return ((at["z"] * 2 + at["yh"]) * 2 + at["c"], at["x"] * 2 + at["yl"])


def ring(me, axis, d):
    at = dict(me)
    if axis == "y":
        to = (me["yh"] * 2 + me["yl"] + d) % 4
        at["yh"], at["yl"] = to // 2, to % 2
    else:
        to = (me[axis] + d) % 4
        at[axis] = to
    return device(at), to


def kernel(tok_h, key_h, gain, win_h, wout_h, g_out, comb_out,
           tok, key, logit, sct, comb, numer, win, wout, aux, auxr, fcol,
           csend, crecv, s1, r1, s2x, s2z, r2x, r2z, ysend, yrecv, gy, g,
           load_sem, comb_sem, send_sem, recv_sem):
    me = place()
    my = me["yh"] * 2 + me["yl"]
    other = dict(me)
    other["c"] = 1 - me["c"]
    partner = device(other)

    key_in = pltpu.make_async_copy(key_h, key, load_sem.at[0])
    key_in.start()
    tok_in = []
    for t in range(TILES):
        rows = pl.ds(t * TILE, TILE)
        tok_in.append(pltpu.make_async_copy(tok_h.at[rows], tok.at[rows], load_sem.at[1 + t]))
        tok_in[-1].start()
    win_in = pltpu.make_async_copy(win_h.at[0], win, load_sem.at[TILES + 1])
    wout_in = pltpu.make_async_copy(wout_h.at[0], wout, load_sem.at[TILES + 2])

    barrier = pltpu.get_barrier_semaphore()
    pl.semaphore_signal(barrier, inc=1, device_id=partner, device_id_type=MESH)
    for axis in "xzy":
        for d in (1, 2, 3):
            pl.semaphore_signal(barrier, inc=1, device_id=ring(me, axis, d)[0], device_id_type=MESH)

    def remote(src, dst, sem, target):
        return pltpu.make_async_remote_copy(
            src_ref=src, dst_ref=dst, send_sem=send_sem.at[sem], recv_sem=recv_sem.at[sem],
            device_id=target, device_id_type=MESH)

    started = []

    def send(src, dst, sem, target):
        copy = remote(src, dst, sem, target)
        copy.start()
        started.append(copy)
        return copy

    key_in.wait()
    peak8 = jnp.full((8, SLOTS), -jnp.inf, F32)
    for t in range(TILES):
        rows = pl.ds(t * TILE, TILE)
        tok_in[t].wait()
        part = jnp.dot(tok[rows], key[...], preferred_element_type=F32)
        logit[rows] = part
        peak8 = jnp.maximum(peak8, jnp.max(part.reshape(TILE // 8, 8, SLOTS), axis=0))
    win_in.start()
    wout_in.start()
    peak = jnp.max(peak8, axis=0, keepdims=True)

    def score_step(t, total8):
        rows = pl.ds(pl.multiple_of(t * TILE, TILE), TILE)
        scores = jnp.exp(logit[rows] - peak)
        sct[:, rows] = scores.T.astype(BF16)
        return total8 + jnp.sum(scores.reshape(TILE // 8, 8, SLOTS), axis=0)

    total8 = lax.fori_loop(0, TILES, score_step, jnp.zeros((8, SLOTS), F32))
    total = jnp.sum(total8, axis=0, keepdims=True)

    row = lax.broadcasted_iota(jnp.int32, (8, SLOTS), 0)

    def put_aux(slot, top, tot):
        aux[slot] = jnp.where(row == 0, top, jnp.where(row == 1, tot, 0.0))

    put_aux(0, peak, total)
    pl.semaphore_wait(barrier, 10)
    send(aux.at[0], auxr.at[0], S_AUX0, partner)

    def merge_aux(own, others, col):
        tops = [own[0:1]] + [o[0:1] for o in others]
        tots = [own[1:2]] + [o[1:2] for o in others]
        top = tops[0]
        for p in tops[1:]:
            top = jnp.maximum(top, p)
        factors = [jnp.exp(p - top) for p in tops]
        tot = factors[0] * tots[0]
        for f, t in zip(factors[1:], tots[1:]):
            tot = tot + f * t
        line = lax.broadcasted_iota(jnp.int32, (128, SLOTS), 0)
        block = jnp.zeros((128, SLOTS), F32)
        for i, f in enumerate(factors):
            block = jnp.where(line == i, f, block)
        fcol[col] = block.T.reshape(4, 2, 2, 4, 8, 128)
        return top, tot

    core_copies, one_copies = {}, {}

    def core_send(k):
        core_copies[k] = send(csend.at[k], crecv.at[k], S_CORE + k, partner)

    def numer_chunk(k, slot):
        cols = pl.ds(k * WIDE, WIDE)
        part = jnp.dot(sct[...], tok[:, cols], preferred_element_type=F32)
        numer[slot] = part.reshape(4, 2, 2, 4, 8, WIDE)
        csend[k] = numer[slot, :, :, 1 - me["c"]].astype(BF16)
        core_send(k)

    def core_merge(k, slot):
        core_copies[k].wait_recv()
        f = fcol[0, :, :, me["c"]]
        both = (numer[slot, :, :, me["c"]] * f[..., 0:1]
                + crecv[k].astype(F32) * f[..., 1:2]).astype(BF16)
        first = k * WIDE < SPLIT
        for i in range(4):
            if first:
                s1[k, i] = both[:, :, i].reshape(8, 8, WIDE)
            else:
                s1[k, i] = both[i].reshape(8, 8, WIDE)
        one_copies[k] = []
        for d in (1, 2, 3):
            target, to = ring(me, "x" if first else "z", d)
            one_copies[k].append(send(s1.at[k, to], r1.at[k, d - 1], S_ONE + 3 * k + d - 1, target))

    aux_one = []
    for i, k in enumerate(ORDER):
        numer_chunk(k, i % 2)
        if i == 0:
            remote(aux.at[0], auxr.at[0], S_AUX0, partner).wait_recv()
            top, tot = merge_aux(aux[0], [auxr[0]], 0)
            put_aux(1, top, tot)
            for j, axis in enumerate("xz"):
                for d in (1, 2, 3):
                    n = 3 * j + d - 1
                    aux_one.append(send(aux.at[1], auxr.at[1 + n], S_AUXA + n, ring(me, axis, d)[0]))
        else:
            core_merge(ORDER[i - 1], (i - 1) % 2)
    core_merge(ORDER[-1], (CHUNKS - 1) % 2)

    for copy in aux_one:
        copy.wait_recv()
    aux_two = []
    for j, axis in enumerate("zx"):
        top, tot = merge_aux(aux[1], [auxr[1 + 3 * j + n] for n in range(3)], 1 + j)
        put_aux(2 + j, top, tot)
        for d in (1, 2, 3):
            n = 3 * j + d - 1
            aux_two.append(send(aux.at[2 + j], auxr.at[7 + n], S_AUXB + n, ring(me, axis, d)[0]))


    def combine_step(t, carry):
        rows = pl.ds(pl.multiple_of(t * TILE, TILE), TILE)
        block = logit[rows]
        e = jnp.exp(block - jnp.max(block, axis=1, keepdims=True))
        comb[rows] = (e / jnp.sum(e, axis=1, keepdims=True)).astype(BF16)
        return carry

    lax.fori_loop(0, TILES, combine_step, 0)
    comb_copy = pltpu.make_async_copy(comb, comb_out, comb_sem.at[0])
    comb_copy.start()

    for copy in aux_two:
        copy.wait_recv()
    for j in range(2):
        top, tot = merge_aux(aux[2 + j], [auxr[7 + 3 * j + n] for n in range(3)], 3 + j)
        if j == 0:
            put_aux(4, top, tot)
    aux_y = [send(aux.at[4], auxr.at[13 + d - 1], S_AUXY + d - 1, ring(me, "y", d)[0]) for d in (1, 2, 3)]

    def stage_one(k):
        first = k * WIDE < SPLIT
        for copy in one_copies[k]:
            copy.wait_recv()
        if first:
            f = fcol[1, :, :, me["c"], me["x"]].reshape(8, 8, 128)
            out = s1[k, me["x"]].astype(F32) * f[..., 0:1]
        else:
            f = fcol[2, me["z"], :, me["c"]].reshape(8, 8, 128)
            out = s1[k, me["z"]].astype(F32) * f[..., 0:1]
        for d in (1, 2, 3):
            out = out + r1[k, d - 1].astype(F32) * f[..., d : d + 1]
        out = out.astype(BF16).reshape((4, 2, 8, WIDE) if first else (2, 4, 8, WIDE))
        at = k * WIDE if first else k * WIDE - SPLIT
        for i in range(4):
            if first:
                s2x[i, :, :, at : at + WIDE] = out[i]
            else:
                s2z[i, :, :, at : at + WIDE] = out[:, i]

    two = []
    for k in (2, 3, 4):
        stage_one(k)
    for d in (1, 2, 3):
        target, to = ring(me, "x", d)
        two.append(send(s2z.at[to], r2z.at[d - 1], S_TWO + 3 + d - 1, target))
    for k in (0, 1):
        stage_one(k)
    for d in (1, 2, 3):
        target, to = ring(me, "z", d)
        two.append(send(s2x.at[to], r2x.at[d - 1], S_TWO + d - 1, target))
    for copy in aux_y:
        copy.wait_recv()
    top, tot = merge_aux(aux[4], [auxr[13 + n] for n in range(3)], 5)
    line = lax.broadcasted_iota(jnp.int32, (128, SLOTS), 0)
    fcol[6] = jnp.where(line == 0, tot, 0.0).T.reshape(4, 2, 2, 4, 8, 128)

    for copy in two:
        copy.wait_recv()
    fx = fcol[3, me["z"], :, me["c"], me["x"]]
    fz = fcol[4, me["z"], :, me["c"], me["x"]]
    outx = s2x[me["z"]].astype(F32) * fx[..., 0:1]
    outz = s2z[me["x"]].astype(F32) * fz[..., 0:1]
    for d in (1, 2, 3):
        outx = outx + r2x[d - 1].astype(F32) * fx[..., d : d + 1]
        outz = outz + r2z[d - 1].astype(F32) * fz[..., d : d + 1]
    ysend[:, :, 0:SPLIT] = outx.astype(BF16)
    ysend[:, :, SPLIT:D] = outz.astype(BF16)

    last = []
    for d in (1, 2, 3):
        target, to = ring(me, "y", d)
        last.append(send(ysend.at[to // 2], yrecv.at[d - 1], S_Y + d - 1, target))
    fy = fcol[5, me["z"], me["yh"], me["c"], me["x"]]
    own_total = fcol[6, me["z"], me["yh"], me["c"], me["x"]]
    slot_in = ysend[me["yh"]].astype(F32) * fy[:, 0:1]
    for copy in last:
        copy.wait_recv()
    for d in (1, 2, 3):
        slot_in = slot_in + yrecv[d - 1].astype(F32) * fy[:, d : d + 1]
    slot_in = slot_in / own_total[:, 0:1]

    normed = (slot_in * gain[...]).astype(BF16)
    win_in.wait()
    wout_in.wait()
    hidden = jax.nn.gelu(jnp.dot(normed, win[...], preferred_element_type=F32)).astype(BF16)
    out = jnp.dot(hidden, wout[...], preferred_element_type=F32)
    half = lax.broadcasted_iota(jnp.int32, (8, D), 0) // 4
    gy[my] = jnp.where(half == me["yl"], out, 0.0).astype(BF16)

    back = []
    for d in (1, 2, 3):
        back.append(send(gy.at[my], gy.at[my], S_GY + d - 1, ring(me, "y", d)[0]))
    for copy in back:
        copy.wait_recv()
    for i in range(2):
        g[me["z"], i, me["c"], me["x"]] = gy[2 * i] + gy[2 * i + 1]
    left, right = pl.ds(0, SPLIT), pl.ds(SPLIT, D - SPLIT)
    g2 = []
    for d in (1, 2, 3):
        mine = g.at[me["z"], :, me["c"], me["x"], :, right]
        g2.append(send(mine, mine, S_G2 + 3 + d - 1, ring(me, "x", d)[0]))
    for d in (1, 2, 3):
        mine = g.at[me["z"], :, me["c"], me["x"], :, left]
        g2.append(send(mine, mine, S_G2 + d - 1, ring(me, "z", d)[0]))
    for copy in g2[0:3]:
        copy.wait_recv()
    g3 = []
    for d in (1, 2, 3):
        mine = g.at[me["z"], :, me["c"], :, :, right]
        g3.append(send(mine, mine, S_G3 + 3 + d - 1, ring(me, "z", d)[0]))
    for copy in g2[3:6]:
        copy.wait_recv()
    for d in (1, 2, 3):
        mine = g.at[:, :, me["c"], me["x"], :, left]
        g3.append(send(mine, mine, S_G3 + d - 1, ring(me, "x", d)[0]))
    gc = []

    def pass_on(d):
        z = (me["z"] + 4 - d) % 4
        x = (me["x"] + 4 - d) % 4
        a = g.at[z, :, me["c"], :, :, right]
        b = g.at[:, :, me["c"], x, :, left]
        gc.append(send(a, a, S_GC + d, partner))
        gc.append(send(b, b, S_GC + 4 + d, partner))

    pass_on(0)
    for d in (1, 2, 3):
        g3[d - 1].wait_recv()
        g3[3 + d - 1].wait_recv()
        pass_on(d)
    for copy in gc:
        copy.wait_recv()
    g_copy = pltpu.make_async_copy(g, g_out, comb_sem.at[1])
    g_copy.start()
    for copy in started:
        copy.wait_send()
    comb_copy.wait()
    g_copy.wait()


def on_device(tokens, slot_keys, norm_gain, w_in, w_out):
    anywhere = pl.BlockSpec(memory_space=pl.ANY)
    vmem = pltpu.VMEM
    gathered, combine = pl.pallas_call(
        kernel,
        out_shape=(
            jax.ShapeDtypeStruct((4, 2, 2, 4, 8, D), BF16),
            jax.ShapeDtypeStruct((TOK, SLOTS), BF16),
        ),
        in_specs=[anywhere, anywhere, pl.BlockSpec(memory_space=vmem), anywhere, anywhere],
        out_specs=(anywhere, anywhere),
        scratch_shapes=[
            vmem((TOK, D), BF16),
            vmem((D, SLOTS), BF16),
            vmem((TOK, SLOTS), F32),
            vmem((SLOTS, TOK), BF16),
            vmem((TOK, SLOTS), BF16),
            vmem((2, 4, 2, 2, 4, 8, WIDE), F32),
            vmem((D, FF), BF16),
            vmem((FF, D), BF16),
            vmem((5, 8, SLOTS), F32),
            vmem((16, 8, SLOTS), F32),
            vmem((7, 4, 2, 2, 4, 8, 128), F32),
            vmem((CHUNKS, 4, 2, 4, 8, WIDE), BF16),
            vmem((CHUNKS, 4, 2, 4, 8, WIDE), BF16),
            vmem((CHUNKS, 4, 8, 8, WIDE), BF16),
            vmem((CHUNKS, 3, 8, 8, WIDE), BF16),
            vmem((4, 2, 8, SPLIT), BF16),
            vmem((4, 2, 8, D - SPLIT), BF16),
            vmem((3, 2, 8, SPLIT), BF16),
            vmem((3, 2, 8, D - SPLIT), BF16),
            vmem((2, 8, D), BF16),
            vmem((3, 8, D), BF16),
            vmem((4, 8, D), BF16),
            vmem((4, 2, 2, 4, 8, D), BF16),
            pltpu.SemaphoreType.DMA((TILES + 3,)),
            pltpu.SemaphoreType.DMA((2,)),
            pltpu.SemaphoreType.DMA((N_SEM,)),
            pltpu.SemaphoreType.DMA((N_SEM,)),
        ],
        compiler_params=pltpu.CompilerParams(
            collective_id=0, has_side_effects=True, vmem_limit_bytes=56 << 20
        ),
        name="route",
    )(tokens, slot_keys, norm_gain, w_in, w_out)
    mixed = jnp.dot(combine, gathered.reshape(SLOTS, D), preferred_element_type=F32)
    return mixed.astype(BF16)


def solution(mesh):
    return jax.shard_map(
        on_device,
        mesh=mesh,
        in_specs=(
            P(("seq", "grp"), None),
            P(),
            P(("seq", "grp"), None),
            P(("seq", "grp"), None, None),
            P(("seq", "grp"), None, None),
        ),
        out_specs=P(("seq", "grp"), None),
        check_vma=False,
    )
```

```python
import jax
import jax.numpy as jnp
from jax import lax
from jax.experimental import pallas as pl
from jax.experimental.pallas import tpu as pltpu
from jax.sharding import PartitionSpec as P

F32 = jnp.float32
BF16 = jnp.bfloat16
MESH = pl.DeviceIdType.MESH
TOK, D, FF, SLOTS = 2048, 1280, 2560, 512
LOADS = (256, 256, 512, 1024)
TILE = 512
COLS = (512, 768)
AUX = 128
FAR_FIRST = (2, 1, 3, 0)


def place():
    seq = lax.axis_index("seq")
    grp = lax.axis_index("grp")
    return seq // 4, (seq // 2) % 2, seq % 2, grp // 2, grp % 2


def split3(v):
    hi = v.astype(BF16).astype(F32)
    mid = (v - hi).astype(BF16).astype(F32)
    lo = (v - hi - mid).astype(BF16).astype(F32)
    return hi, mid, lo


def kernel(tok_h, key, gain, win_h, wout_h, g_out, comb_out,
           tok, logit, sct, comb, numer_a, numer_b, win, wout, aux, fcol, fb,
           csend_a, csend_b, crecv_a, crecv_b, sa, sb, ra, rb, x8, gs, g, gf,
           load_sem, out_sem, pair_send, pair_recv, sum_send, sum_recv, row_send, row_recv):
    z, yh, c, x, yl = place()
    y = yh * 2 + yl
    partner = ((z * 2 + yh) * 2 + 1 - c, x * 2 + yl)

    tok_in, at = [], 0
    for i, n in enumerate(LOADS):
        rows = pl.ds(at, n)
        tok_in.append(pltpu.make_async_copy(tok_h.at[rows], tok.at[rows], load_sem.at[i]))
        tok_in[-1].start()
        at += n
    win_in = pltpu.make_async_copy(win_h.at[0], win, load_sem.at[4])
    wout_in = pltpu.make_async_copy(wout_h.at[0], wout, load_sem.at[5])

    def chip(dz, j):
        tz, ty, tx = (z + dz) % 4, (y + j // 4) % 4, (x + j % 4) % 4
        return tz, ty // 2, tx, ty % 2

    def core_of(tz, tyh, tx, tyl):
        return (tz * 2 + tyh) * 2 + c, tx * 2 + tyl

    def every_chip(act):
        for dz in FAR_FIRST:
            def step(j, carry, dz=dz):
                act(dz, j)
                return carry
            lax.fori_loop(0 if dz else 1, 16, step, 0)

    barrier = pltpu.get_barrier_semaphore()
    pl.semaphore_signal(barrier, inc=1, device_id=partner, device_id_type=MESH)

    def greet(dz, j):
        pl.semaphore_signal(barrier, inc=1, device_id=core_of(*chip(dz, j)), device_id_type=MESH)

    every_chip(greet)

    def pair(src, dst, i):
        return pltpu.make_async_remote_copy(
            src_ref=src, dst_ref=dst, send_sem=pair_send.at[i], recv_sem=pair_recv.at[i],
            device_id=partner, device_id_type=MESH)

    peak8 = jnp.full((8, SLOTS), -jnp.inf, F32)
    at = 0
    for i, n in enumerate(LOADS):
        rows = pl.ds(at, n)
        tok_in[i].wait()
        part = jnp.dot(tok[rows], key[...], preferred_element_type=F32)
        logit[rows] = part
        peak8 = jnp.maximum(peak8, jnp.max(part.reshape(n // 8, 8, SLOTS), axis=0))
        at += n
    win_in.start()
    wout_in.start()
    peak = jnp.max(peak8, axis=0, keepdims=True)

    def score_step(t, total8):
        rows = pl.ds(pl.multiple_of(t * TILE, TILE), TILE)
        scores = jnp.exp(logit[rows] - peak)
        sct[:, rows] = scores.astype(BF16).T
        return total8 + jnp.sum(scores.reshape(TILE // 8, 8, SLOTS), axis=0)

    total8 = lax.fori_loop(0, TOK // TILE, score_step, jnp.zeros((8, SLOTS), F32))
    total = jnp.sum(total8, axis=0, keepdims=True)
    row = lax.broadcasted_iota(jnp.int32, (8, SLOTS), 0)
    aux[0] = jnp.where(row == 0, peak, jnp.where(row == 1, total, 0.0))
    pl.semaphore_wait(barrier, 64)
    copies = [pair(aux.at[0], aux.at[1], 0)]
    copies[0].start()

    def numer_part(cols, numer, csend, crecv, i):
        part = jnp.dot(sct[...], tok[:, cols], preferred_element_type=F32)
        numer[...] = part.reshape(numer.shape)
        csend[...] = numer[:, :, 1 - c].astype(BF16)
        copies.append(pair(csend, crecv, i))
        copies[i].start()

    numer_part(pl.ds(0, COLS[0]), numer_a, csend_a, crecv_a, 1)

    copies[0].wait_recv()
    tops, tots = (peak, aux[1][0:1]), (total, aux[1][1:2])
    top = jnp.maximum(*tops)
    factors = [jnp.exp(p - top) for p in tops]
    tot = factors[0] * tots[0] + factors[1] * tots[1]
    line = lax.broadcasted_iota(jnp.int32, (AUX, SLOTS), 0)
    block = jnp.zeros((AUX, SLOTS), F32)
    for i, v in enumerate(split3(top) + split3(tot) + tuple(factors)):
        block = jnp.where(line == i, v, block)
    fcol[...] = block.T.reshape(4, 2, 2, 4, 8, AUX)

    numer_part(pl.ds(COLS[0], COLS[1]), numer_b, csend_b, crecv_b, 2)

    def sum_copy(src, dst, i, target):
        return pltpu.make_async_remote_copy(
            src_ref=src, dst_ref=dst, send_sem=sum_send.at[i], recv_sem=sum_recv.at[i],
            device_id=target, device_id_type=MESH)

    def pair_sum(numer, crecv, s, r, i, n):
        copies[i].wait_recv()

        def step(tz, carry):
            f = fcol[tz, :, c]
            both = numer[tz, :, c] * f[..., 6:7] + crecv[tz].astype(F32) * f[..., 7:8]
            for h in range(2):
                s[tz, :, :, h, :, 0:n] = both[:, :, 4 * h : 4 * h + 4].astype(BF16)
                if i == 1:
                    s[tz, :, :, h, :, n : n + AUX] = f[:, :, 4 * h : 4 * h + 4].astype(BF16)
            return carry

        lax.fori_loop(0, 4, step, 0)

        def give(dz, j):
            to = chip(dz, j)
            sum_copy(s.at[to], r.at[dz * 16 + j], i - 1, core_of(*to)).start()

        every_chip(give)
        pltpu.make_async_copy(s.at[z, yh, x, yl], r.at[0], sum_recv.at[i - 1]).start()

    pair_sum(numer_a, crecv_a, sa, ra, 1, COLS[0])
    pair_sum(numer_b, crecv_b, sb, rb, 2, COLS[1])

    def combine_step(t, carry):
        rows = pl.ds(pl.multiple_of(t * 256, 256), 256)
        e = logit[rows]
        e = jnp.exp(e - jnp.max(e, axis=1, keepdims=True))
        comb[rows] = (e / jnp.sum(e, axis=1, keepdims=True)).astype(BF16)
        return carry

    lax.fori_loop(0, TOK // 256, combine_step, 0)
    comb_copy = pltpu.make_async_copy(comb, comb_out, out_sem.at[0])
    comb_copy.start()

    sum_copy(ra, ra, 0, partner).wait_recv()
    a = ra[:, :, COLS[0] : COLS[0] + AUX].astype(F32)
    tops = a[..., 0:1] + a[..., 1:2] + a[..., 2:3]
    tots = a[..., 3:4] + a[..., 4:5] + a[..., 5:6]
    factor = jnp.exp(tops - jnp.max(tops, axis=0, keepdims=True))
    own_total = jnp.sum(factor * tots, axis=0)
    fb[...] = jnp.broadcast_to(factor, fb.shape)
    own_total = jnp.broadcast_to(own_total, (4, 128))

    def gather_sum(r, k, to):
        cols = pl.ds(k * 128, 128)
        x8[0:4, to : to + 128] = jnp.sum(r[:, :, cols].astype(F32) * fb[...], axis=0) / own_total

    x8[4:8] = jnp.zeros((4, D), F32)
    for k in range(COLS[0] // 128):
        gather_sum(ra, k, k * 128)
    sum_copy(rb, rb, 1, partner).wait_recv()
    for k in range(COLS[1] // 128):
        gather_sum(rb, k, COLS[0] + k * 128)

    normed = (x8[...] * gain[...]).astype(BF16)
    win_in.wait()
    wout_in.wait()
    hidden = jax.nn.gelu(jnp.dot(normed, win[...], preferred_element_type=F32)).astype(BF16)
    gs[...] = jnp.dot(hidden, wout[...], preferred_element_type=F32)[0:4].astype(BF16)

    def row_copy(src, dst, i, target):
        return pltpu.make_async_remote_copy(
            src_ref=src, dst_ref=dst, send_sem=row_send.at[i], recv_sem=row_recv.at[i],
            device_id=target, device_id_type=MESH)

    def show(dz, j):
        row_copy(gs, g.at[z, yh, c, x, yl], dz, core_of(*chip(dz, j))).start()

    every_chip(show)
    pltpu.make_async_copy(gs, g.at[z, yh, c, x, yl], row_recv.at[0]).start()
    for dz in FAR_FIRST:
        slab = g.at[(z + 4 - dz) % 4, :, c]
        row_copy(slab, slab, dz, partner).wait_recv()
        copies.append(pair(slab, slab, 3 + dz))
        copies[-1].start()
    g_copies = []
    for i, dz in enumerate(FAR_FIRST):
        tz = (z + 4 - dz) % 4
        copies[3 + i].wait_recv()
        gf[tz] = g[tz].reshape(128, D)
        g_copies.append(pltpu.make_async_copy(gf.at[tz], g_out.at[tz], out_sem.at[1 + i]))
        g_copies[-1].start()

    for copy in copies:
        copy.wait_send()
    sum_copy(ra.at[pl.ds(0, 63)], ra.at[pl.ds(0, 63)], 0, partner).wait_send()
    sum_copy(rb.at[pl.ds(0, 63)], rb.at[pl.ds(0, 63)], 1, partner).wait_send()
    slab = g.at[0, :, 0]
    for dz in (1, 2, 3):
        row_copy(slab, slab, dz, partner).wait_send()
    part = ra.at[pl.ds(0, 30)]
    row_copy(part, part, 0, partner).wait_send()
    comb_copy.wait()
    for copy in g_copies:
        copy.wait()


def mix_kernel(comb, rows, out):
    out[...] = jnp.dot(comb[...], rows[...], preferred_element_type=F32).astype(BF16)


def on_device(tokens, slot_keys, norm_gain, w_in, w_out):
    anywhere = pl.BlockSpec(memory_space=pl.ANY)
    held = pl.BlockSpec(memory_space=pltpu.VMEM)
    vmem = pltpu.VMEM
    sem = pltpu.SemaphoreType.DMA
    gathered, combine = pl.pallas_call(
        kernel,
        out_shape=(
            jax.ShapeDtypeStruct((4, 128, D), BF16),
            jax.ShapeDtypeStruct((TOK, SLOTS), BF16),
        ),
        in_specs=[anywhere, held, held, anywhere, anywhere],
        out_specs=(anywhere, anywhere),
        scratch_shapes=[
            vmem((TOK, D), BF16),
            vmem((TOK, SLOTS), F32),
            vmem((SLOTS, TOK), BF16),
            vmem((TOK, SLOTS), BF16),
            vmem((4, 2, 2, 4, 8, COLS[0]), F32),
            vmem((4, 2, 2, 4, 8, COLS[1]), F32),
            vmem((D, FF), BF16),
            vmem((FF, D), BF16),
            vmem((2, 8, SLOTS), F32),
            vmem((4, 2, 2, 4, 8, AUX), F32),
            vmem((64, 4, 128), F32),
            vmem((4, 2, 4, 8, COLS[0]), BF16),
            vmem((4, 2, 4, 8, COLS[1]), BF16),
            vmem((4, 2, 4, 8, COLS[0]), BF16),
            vmem((4, 2, 4, 8, COLS[1]), BF16),
            vmem((4, 2, 4, 2, 4, COLS[0] + AUX), BF16),
            vmem((4, 2, 4, 2, 4, COLS[1]), BF16),
            vmem((64, 4, COLS[0] + AUX), BF16),
            vmem((64, 4, COLS[1]), BF16),
            vmem((8, D), F32),
            vmem((4, D), BF16),
            vmem((4, 2, 2, 4, 2, 4, D), BF16),
            vmem((4, 128, D), BF16),
            sem((6,)),
            sem((5,)),
            sem((7,)),
            sem((7,)),
            sem((2,)),
            sem((2,)),
            sem((4,)),
            sem((4,)),
        ],
        compiler_params=pltpu.CompilerParams(
            collective_id=0, has_side_effects=True, vmem_limit_bytes=48 << 20
        ),
        name="route",
    )(tokens, slot_keys, norm_gain, w_in, w_out)
    rows = 256
    return pl.pallas_call(
        mix_kernel,
        out_shape=jax.ShapeDtypeStruct((TOK, D), BF16),
        grid=(TOK // rows,),
        in_specs=[
            pl.BlockSpec((rows, SLOTS), lambda i: (i, 0)),
            pl.BlockSpec((SLOTS, D), lambda i: (0, 0)),
        ],
        out_specs=pl.BlockSpec((rows, D), lambda i: (i, 0)),
        compiler_params=pltpu.CompilerParams(vmem_limit_bytes=12 << 20),
        name="mix",
    )(combine, gathered.reshape(SLOTS, D))


def solution(mesh):
    return jax.shard_map(
        on_device,
        mesh=mesh,
        in_specs=(
            P(("seq", "grp"), None),
            P(),
            P(("seq", "grp"), None),
            P(("seq", "grp"), None, None),
            P(("seq", "grp"), None, None),
        ),
        out_specs=P(("seq", "grp"), None),
        check_vma=False,
    )
```

```python
import jax
import jax.numpy as jnp
from jax import lax
from jax.experimental import pallas as pl
from jax.experimental.pallas import tpu as pltpu
from jax.sharding import PartitionSpec as P

F32 = jnp.float32
BF16 = jnp.bfloat16
MESH = pl.DeviceIdType.MESH
TOK, D, FF, SLOTS = 2048, 1280, 2560, 512
LOADS = (256, 256, 512, 1024)
TILE = 512
COLS = (256, 512, 512)
START = (0, 256, 768)
AUX = 128
FAR_FIRST = (2, 1, 3, 0)


def place():
    seq = lax.axis_index("seq")
    grp = lax.axis_index("grp")
    return seq // 4, (seq // 2) % 2, seq % 2, grp // 2, grp % 2


def split3(v):
    hi = v.astype(BF16).astype(F32)
    mid = (v - hi).astype(BF16).astype(F32)
    lo = (v - hi - mid).astype(BF16).astype(F32)
    return hi, mid, lo


def kernel(tok_h, key, gain_h, win_h, wout_h, g_out, comb_out,
           tok, logit, sct, comb, numer_a, numer_b, numer_c, gain, win, wout, aux, fcol, fb,
           csend_a, csend_b, csend_c, crecv_a, crecv_b, crecv_c, sa, sb, sc, ra, rb, rc, x8, gs, g, gf,
           in_sem, load_sem, out_sem, pair_send, pair_recv, sum_send, sum_recv, row_send, row_recv):
    z, yh, c, x, yl = place()
    y = yh * 2 + yl
    partner = ((z * 2 + yh) * 2 + 1 - c, x * 2 + yl)

    tok_in, at = [], 0
    for i, n in enumerate(LOADS):
        rows = pl.ds(at, n)
        tok_in.append(pltpu.make_async_copy(tok_h.at[rows], tok.at[rows], load_sem.at[i]))
        tok_in[-1].start()
        at += n
    gain_in = pltpu.make_async_copy(gain_h, gain, load_sem.at[6])
    win_in = pltpu.make_async_copy(win_h.at[0], win, load_sem.at[4])
    wout_in = pltpu.make_async_copy(wout_h.at[0], wout, load_sem.at[5])

    def chip(dz, j):
        tz, ty, tx = (z + dz) % 4, (y + j // 4) % 4, (x + j % 4) % 4
        return tz, ty // 2, tx, ty % 2

    def core_of(tz, tyh, tx, tyl):
        return (tz * 2 + tyh) * 2 + c, tx * 2 + tyl

    def every_chip(act):
        for dz in FAR_FIRST:
            def step(j, carry, dz=dz):
                act(dz, j)
                return carry
            lax.fori_loop(0 if dz else 1, 16, step, 0)

    barrier = pltpu.get_barrier_semaphore()
    pl.semaphore_signal(barrier, inc=1, device_id=partner, device_id_type=MESH)

    def line(axis, d):
        if axis == "x":
            return core_of(z, yh, (x + d) % 4, yl)
        if axis == "y":
            ty = (y + d) % 4
            return core_of(z, ty // 2, x, ty % 2)
        return core_of((z + d) % 4, yh, x, yl)

    def greet(sem, axes):
        for axis in axes:
            for d in (1, 2, 3):
                pl.semaphore_signal(sem, inc=1, device_id=line(axis, d), device_id_type=MESH)

    greet(barrier, "xyz")

    def pair(src, dst, i):
        return pltpu.make_async_remote_copy(
            src_ref=src, dst_ref=dst, send_sem=pair_send.at[i], recv_sem=pair_recv.at[i],
            device_id=partner, device_id_type=MESH)

    peak8 = jnp.full((8, SLOTS), -jnp.inf, F32)
    at = 0
    for i, n in enumerate(LOADS):
        rows = pl.ds(at, n)
        tok_in[i].wait()
        part = jnp.dot(tok[rows], key[...], preferred_element_type=F32)
        logit[rows] = part
        peak8 = jnp.maximum(peak8, jnp.max(part.reshape(n // 8, 8, SLOTS), axis=0))
        at += n
        if i == 1:
            pl.semaphore_wait(barrier, 10)
            greet(in_sem.at[0], "y")
        if i == 2:
            pl.semaphore_wait(in_sem.at[0], 3)
            greet(in_sem.at[1], "z")
    win_in.start()
    wout_in.start()
    gain_in.start()
    peak = jnp.max(peak8, axis=0, keepdims=True)

    def score_step(t, total8):
        rows = pl.ds(pl.multiple_of(t * TILE, TILE), TILE)
        scores = jnp.exp(logit[rows] - peak)
        sct[:, rows] = scores.astype(BF16).T
        return total8 + jnp.sum(scores.reshape(TILE // 8, 8, SLOTS), axis=0)

    total8 = lax.fori_loop(0, TOK // TILE, score_step, jnp.zeros((8, SLOTS), F32))
    total = jnp.sum(total8, axis=0, keepdims=True)
    row = lax.broadcasted_iota(jnp.int32, (8, SLOTS), 0)
    aux[0] = jnp.where(row == 0, peak, jnp.where(row == 1, total, 0.0))
    copies = [pair(aux.at[0], aux.at[1], 0)]
    copies[0].start()

    def numer_part(cols, numer, csend, crecv, i):
        part = jnp.dot(sct[...], tok[:, cols], preferred_element_type=F32)
        numer[...] = part.reshape(numer.shape)
        csend[...] = numer[:, :, 1 - c].astype(BF16)
        copies.append(pair(csend, crecv, i))
        copies[i].start()

    parts = ((numer_a, csend_a, crecv_a, sa, ra), (numer_b, csend_b, crecv_b, sb, rb), (numer_c, csend_c, crecv_c, sc, rc))
    for i in range(2):
        numer_part(pl.ds(START[i], COLS[i]), *parts[i][:3], i + 1)

    copies[0].wait_recv()
    tops, tots = (peak, aux[1][0:1]), (total, aux[1][1:2])
    top = jnp.maximum(*tops)
    factors = [jnp.exp(p - top) for p in tops]
    tot = factors[0] * tots[0] + factors[1] * tots[1]
    line = lax.broadcasted_iota(jnp.int32, (AUX, SLOTS), 0)
    block = jnp.zeros((AUX, SLOTS), F32)
    for i, v in enumerate(split3(top) + split3(tot) + tuple(factors)):
        block = jnp.where(line == i, v, block)
    fcol[...] = block.T.reshape(4, 2, 2, 4, 8, AUX)

    def sum_copy(src, dst, i, target):
        return pltpu.make_async_remote_copy(
            src_ref=src, dst_ref=dst, send_sem=sum_send.at[i], recv_sem=sum_recv.at[i],
            device_id=target, device_id_type=MESH)

    def pair_sum(numer, crecv, s, r, i, n):
        copies[i].wait_recv()

        def step(tz, carry):
            f = fcol[tz, :, c]
            both = numer[tz, :, c] * f[..., 6:7] + crecv[tz].astype(F32) * f[..., 7:8]
            for h in range(2):
                s[tz, :, :, h, :, 0:n] = both[:, :, 4 * h : 4 * h + 4].astype(BF16)
                if i == 1:
                    s[tz, :, :, h, :, n : n + AUX] = f[:, :, 4 * h : 4 * h + 4].astype(BF16)
            return carry

        lax.fori_loop(0, 4, step, 0)

        def give(dz, j):
            to = chip(dz, j)
            sum_copy(s.at[to], r.at[dz * 16 + j], i - 1, core_of(*to)).start()

        every_chip(give)
        pltpu.make_async_copy(s.at[z, yh, x, yl], r.at[0], sum_recv.at[i - 1]).start()

    pl.semaphore_wait(in_sem.at[1], 3)
    pair_sum(numer_a, *parts[0][2:], 1, COLS[0])
    numer_part(pl.ds(START[2], COLS[2]), *parts[2][:3], 3)
    pair_sum(numer_b, *parts[1][2:], 2, COLS[1])
    pair_sum(numer_c, *parts[2][2:], 3, COLS[2])

    def combine_step(t, carry):
        rows = pl.ds(pl.multiple_of(t * 256, 256), 256)
        e = logit[rows]
        e = jnp.exp(e - jnp.max(e, axis=1, keepdims=True))
        comb[rows] = (e / jnp.sum(e, axis=1, keepdims=True)).astype(BF16)
        return carry

    lax.fori_loop(0, TOK // 256, combine_step, 0)
    comb_copy = pltpu.make_async_copy(comb, comb_out, out_sem.at[0])
    comb_copy.start()

    sum_copy(ra, ra, 0, partner).wait_recv()
    a = ra[:, :, COLS[0] : COLS[0] + AUX].astype(F32)
    tops = a[..., 0:1] + a[..., 1:2] + a[..., 2:3]
    tots = a[..., 3:4] + a[..., 4:5] + a[..., 5:6]
    factor = jnp.exp(tops - jnp.max(tops, axis=0, keepdims=True))
    own_total = jnp.sum(factor * tots, axis=0)
    fb[...] = jnp.broadcast_to(factor, fb.shape)
    own_total = jnp.broadcast_to(own_total, (4, 128))

    def gather_sum(r, k, to):
        cols = pl.ds(k * 128, 128)
        x8[0:4, to : to + 128] = jnp.sum(r[:, :, cols].astype(F32) * fb[...], axis=0) / own_total

    x8[4:8] = jnp.zeros((4, D), F32)
    for i, r in enumerate((ra, rb, rc)):
        if i:
            sum_copy(r, r, i, partner).wait_recv()
        for k in range(COLS[i] // 128):
            gather_sum(r, k, START[i] + k * 128)

    gain_in.wait()
    normed = (x8[...] * gain[...]).astype(BF16)
    win_in.wait()
    wout_in.wait()
    hidden = jax.nn.gelu(jnp.dot(normed, win[...], preferred_element_type=F32)).astype(BF16)
    gs[...] = jnp.dot(hidden, wout[...], preferred_element_type=F32)[0:4].astype(BF16)

    def row_copy(src, dst, i, target):
        return pltpu.make_async_remote_copy(
            src_ref=src, dst_ref=dst, send_sem=row_send.at[i], recv_sem=row_recv.at[i],
            device_id=target, device_id_type=MESH)

    def show(dz, j):
        row_copy(gs, g.at[z, yh, c, x, yl], dz, core_of(*chip(dz, j))).start()

    every_chip(show)
    pltpu.make_async_copy(gs, g.at[z, yh, c, x, yl], row_recv.at[0]).start()
    for dz in FAR_FIRST:
        slab = g.at[(z + 4 - dz) % 4, :, c]
        row_copy(slab, slab, dz, partner).wait_recv()
        copies.append(pair(slab, slab, 4 + dz))
        copies[-1].start()
    g_copies = []
    for i, dz in enumerate(FAR_FIRST):
        tz = (z + 4 - dz) % 4
        copies[4 + i].wait_recv()
        gf[tz] = g[tz].reshape(128, D)
        g_copies.append(pltpu.make_async_copy(gf.at[tz], g_out.at[tz], out_sem.at[1 + i]))
        g_copies[-1].start()

    for copy in copies:
        copy.wait_send()
    for i, r in enumerate((ra, rb, rc)):
        sent = r.at[pl.ds(0, 63)]
        sum_copy(sent, sent, i, partner).wait_send()
    slab = g.at[0, :, 0]
    for dz in (1, 2, 3):
        row_copy(slab, slab, dz, partner).wait_send()
    part = ra.at[pl.ds(0, 50)]
    row_copy(part, part, 0, partner).wait_send()
    comb_copy.wait()
    for copy in g_copies:
        copy.wait()


def mix_kernel(comb, rows, out, held, sem):
    copies = []
    for k, (at, n) in enumerate(((0, TOK), (0, TOK), (0, TOK), (0, TOK), (0, TOK // 2), (TOK // 2, TOK // 2))):
        block = (pl.ds(at, n), pl.ds(min(k, 4) * 256, 256))
        held[block] = jnp.dot(comb[block[0]], rows[:, block[1]], preferred_element_type=F32).astype(BF16)
        copies.append(pltpu.make_async_copy(held.at[block], out.at[block], sem.at[k]))
        copies[k].start()
    for copy in copies:
        copy.wait()


def on_device(tokens, slot_keys, norm_gain, w_in, w_out):
    anywhere = pl.BlockSpec(memory_space=pl.ANY)
    held = pl.BlockSpec(memory_space=pltpu.VMEM)
    vmem = pltpu.VMEM
    sem = pltpu.SemaphoreType.DMA
    gathered, combine = pl.pallas_call(
        kernel,
        out_shape=(
            jax.ShapeDtypeStruct((4, 128, D), BF16),
            jax.ShapeDtypeStruct((TOK, SLOTS), BF16),
        ),
        in_specs=[anywhere, held, anywhere, anywhere, anywhere],
        out_specs=(anywhere, anywhere),
        scratch_shapes=[
            vmem((TOK, D), BF16),
            vmem((TOK, SLOTS), F32),
            vmem((SLOTS, TOK), BF16),
            vmem((TOK, SLOTS), BF16),
            *(vmem((4, 2, 2, 4, 8, n), F32) for n in COLS),
            vmem((1, D), F32),
            vmem((D, FF), BF16),
            vmem((FF, D), BF16),
            vmem((2, 8, SLOTS), F32),
            vmem((4, 2, 2, 4, 8, AUX), F32),
            vmem((64, 4, 128), F32),
            *(vmem((4, 2, 4, 8, n), BF16) for n in COLS),
            *(vmem((4, 2, 4, 8, n), BF16) for n in COLS),
            *(vmem((4, 2, 4, 2, 4, n), BF16) for n in (COLS[0] + AUX, COLS[1], COLS[2])),
            *(vmem((64, 4, n), BF16) for n in (COLS[0] + AUX, COLS[1], COLS[2])),
            vmem((8, D), F32),
            vmem((4, D), BF16),
            vmem((4, 2, 2, 4, 2, 4, D), BF16),
            vmem((4, 128, D), BF16),
            pltpu.SemaphoreType.REGULAR((2,)),
            sem((7,)),
            sem((5,)),
            sem((8,)),
            sem((8,)),
            sem((3,)),
            sem((3,)),
            sem((4,)),
            sem((4,)),
        ],
        compiler_params=pltpu.CompilerParams(
            collective_id=0, has_side_effects=True, vmem_limit_bytes=48 << 20
        ),
        name="route",
    )(tokens, slot_keys, norm_gain, w_in, w_out)
    return pl.pallas_call(
        mix_kernel,
        out_shape=jax.ShapeDtypeStruct((TOK, D), BF16),
        in_specs=[held, held],
        out_specs=anywhere,
        scratch_shapes=[vmem((TOK, D), BF16), sem((6,))],
        compiler_params=pltpu.CompilerParams(vmem_limit_bytes=12 << 20),
        name="mix",
    )(combine, gathered.reshape(SLOTS, D))


def solution(mesh):
    return jax.shard_map(
        on_device,
        mesh=mesh,
        in_specs=(
            P(("seq", "grp"), None),
            P(),
            P(("seq", "grp"), None),
            P(("seq", "grp"), None, None),
            P(("seq", "grp"), None, None),
        ),
        out_specs=P(("seq", "grp"), None),
        check_vma=False,
    )
```

```python
import jax
import jax.numpy as jnp
from jax import lax
from jax.experimental import pallas as pl
from jax.experimental.pallas import tpu as pltpu
from jax.sharding import PartitionSpec as P

F32 = jnp.float32
BF16 = jnp.bfloat16
MESH = pl.DeviceIdType.MESH
TOK, D, FF, SLOTS = 2048, 1280, 2560, 512
LOADS = (256, 256, 512, 1024)
TILE = 512
COLS = (256, 512, 512)
START = (0, 256, 768)
AUX = 128
BACK = (768, 512)
FAR_FIRST = (2, 1, 3, 0)


def place():
    seq = lax.axis_index("seq")
    grp = lax.axis_index("grp")
    return seq // 4, (seq // 2) % 2, seq % 2, grp // 2, grp % 2


def split3(v):
    hi = v.astype(BF16).astype(F32)
    mid = (v - hi).astype(BF16).astype(F32)
    lo = (v - hi - mid).astype(BF16).astype(F32)
    return hi, mid, lo


def kernel(tok_h, key_h, gain_h, win_h, wout_h, g_out, comb_out, mix_out,
           tok, key, logit, sct, comb, numer_a, numer_b, numer_c, gain, win, wout, aux, fcol, fb,
           csend_a, csend_b, csend_c, crecv_a, crecv_b, crecv_c, sa, sb, sc, ra, rb, rc, x8, gs_a, gs_b, ga, gb, fa, fb_rows,
           in_sem, load_sem, out_sem, pair_send, pair_recv, sum_send, sum_recv, row_send, row_recv):
    z, yh, c, x, yl = place()
    y = yh * 2 + yl
    partner = ((z * 2 + yh) * 2 + 1 - c, x * 2 + yl)

    key_in = pltpu.make_async_copy(key_h, key, load_sem.at[7])
    key_in.start()
    tok_in, at = [], 0
    for i, n in enumerate(LOADS):
        rows = pl.ds(at, n)
        tok_in.append(pltpu.make_async_copy(tok_h.at[rows], tok.at[rows], load_sem.at[i]))
        tok_in[-1].start()
        at += n
    gain_in = pltpu.make_async_copy(gain_h, gain, load_sem.at[6])
    win_in = pltpu.make_async_copy(win_h.at[0], win, load_sem.at[4])
    wout_in = pltpu.make_async_copy(wout_h.at[0], wout, load_sem.at[5])

    def chip(dz, j):
        tz, ty, tx = (z + dz) % 4, (y + j // 4) % 4, (x + j % 4) % 4
        return tz, ty // 2, tx, ty % 2

    def core_of(tz, tyh, tx, tyl):
        return (tz * 2 + tyh) * 2 + c, tx * 2 + tyl

    def every_chip(act):
        for dz in FAR_FIRST:
            def step(j, carry, dz=dz):
                act(dz, j)
                return carry
            lax.fori_loop(0 if dz else 1, 16, step, 0)

    barrier = pltpu.get_barrier_semaphore()
    pl.semaphore_signal(barrier, inc=1, device_id=partner, device_id_type=MESH)

    def line(axis, d):
        if axis == "x":
            return core_of(z, yh, (x + d) % 4, yl)
        if axis == "y":
            ty = (y + d) % 4
            return core_of(z, ty // 2, x, ty % 2)
        return core_of((z + d) % 4, yh, x, yl)

    def greet(sem, axes):
        for axis in axes:
            for d in (1, 2, 3):
                pl.semaphore_signal(sem, inc=1, device_id=line(axis, d), device_id_type=MESH)

    greet(barrier, "xyz")

    def pair(src, dst, i):
        return pltpu.make_async_remote_copy(
            src_ref=src, dst_ref=dst, send_sem=pair_send.at[i], recv_sem=pair_recv.at[i],
            device_id=partner, device_id_type=MESH)

    key_in.wait()
    peak8 = jnp.full((8, SLOTS), -jnp.inf, F32)
    at = 0
    for i, n in enumerate(LOADS):
        rows = pl.ds(at, n)
        tok_in[i].wait()
        part = jnp.dot(tok[rows], key[...], preferred_element_type=F32)
        logit[rows] = part
        peak8 = jnp.maximum(peak8, jnp.max(part.reshape(n // 8, 8, SLOTS), axis=0))
        at += n
        if i == 1:
            pl.semaphore_wait(barrier, 10)
            greet(in_sem.at[0], "y")
        if i == 2:
            pl.semaphore_wait(in_sem.at[0], 3)
            greet(in_sem.at[1], "z")
    win_in.start()
    wout_in.start()
    gain_in.start()
    peak = jnp.max(peak8, axis=0, keepdims=True)

    def score_step(t, total8):
        rows = pl.ds(pl.multiple_of(t * TILE, TILE), TILE)
        scores = jnp.exp(logit[rows] - peak)
        sct[:, rows] = scores.astype(BF16).T
        return total8 + jnp.sum(scores.reshape(TILE // 8, 8, SLOTS), axis=0)

    total8 = lax.fori_loop(0, TOK // TILE, score_step, jnp.zeros((8, SLOTS), F32))
    total = jnp.sum(total8, axis=0, keepdims=True)
    row = lax.broadcasted_iota(jnp.int32, (8, SLOTS), 0)
    aux[0] = jnp.where(row == 0, peak, jnp.where(row == 1, total, 0.0))
    copies = [pair(aux.at[0], aux.at[1], 0)]
    copies[0].start()

    def numer_part(cols, numer, csend, crecv, i):
        part = jnp.dot(sct[...], tok[:, cols], preferred_element_type=F32)
        numer[...] = part.reshape(numer.shape)
        csend[...] = numer[:, :, 1 - c].astype(BF16)
        copies.append(pair(csend, crecv, i))
        copies[i].start()

    parts = ((numer_a, csend_a, crecv_a, sa, ra), (numer_b, csend_b, crecv_b, sb, rb), (numer_c, csend_c, crecv_c, sc, rc))
    for i in range(2):
        numer_part(pl.ds(START[i], COLS[i]), *parts[i][:3], i + 1)

    copies[0].wait_recv()
    tops, tots = (peak, aux[1][0:1]), (total, aux[1][1:2])
    top = jnp.maximum(*tops)
    factors = [jnp.exp(p - top) for p in tops]
    tot = factors[0] * tots[0] + factors[1] * tots[1]
    line = lax.broadcasted_iota(jnp.int32, (AUX, SLOTS), 0)
    block = jnp.zeros((AUX, SLOTS), F32)
    for i, v in enumerate(split3(top) + split3(tot) + tuple(factors)):
        block = jnp.where(line == i, v, block)
    fcol[...] = block.T.reshape(4, 2, 2, 4, 8, AUX)

    def sum_copy(src, dst, i, target):
        return pltpu.make_async_remote_copy(
            src_ref=src, dst_ref=dst, send_sem=sum_send.at[i], recv_sem=sum_recv.at[i],
            device_id=target, device_id_type=MESH)

    def pair_sum(numer, crecv, s, r, i, n):
        copies[i].wait_recv()

        def step(tz, carry):
            f = fcol[tz, :, c]
            both = numer[tz, :, c] * f[..., 6:7] + crecv[tz].astype(F32) * f[..., 7:8]
            for h in range(2):
                s[tz, :, :, h, :, 0:n] = both[:, :, 4 * h : 4 * h + 4].astype(BF16)
                if i == 1:
                    s[tz, :, :, h, :, n : n + AUX] = f[:, :, 4 * h : 4 * h + 4].astype(BF16)
            return carry

        lax.fori_loop(0, 4, step, 0)

        def give(dz, j):
            to = chip(dz, j)
            sum_copy(s.at[to], r.at[dz * 16 + j], i - 1, core_of(*to)).start()

        every_chip(give)
        pltpu.make_async_copy(s.at[z, yh, x, yl], r.at[0], sum_recv.at[i - 1]).start()

    pl.semaphore_wait(in_sem.at[1], 3)
    pair_sum(numer_a, *parts[0][2:], 1, COLS[0])
    numer_part(pl.ds(START[2], COLS[2]), *parts[2][:3], 3)
    pair_sum(numer_b, *parts[1][2:], 2, COLS[1])
    pair_sum(numer_c, *parts[2][2:], 3, COLS[2])

    def combine_step(t, carry):
        rows = pl.ds(pl.multiple_of(t * 256, 256), 256)
        e = logit[rows]
        e = jnp.exp(e - jnp.max(e, axis=1, keepdims=True))
        comb[rows] = (e / jnp.sum(e, axis=1, keepdims=True)).astype(BF16)
        return carry

    lax.fori_loop(0, TOK // 256, combine_step, 0)
    comb_copy = pltpu.make_async_copy(comb, comb_out, out_sem.at[0])
    comb_copy.start()

    sum_copy(ra, ra, 0, partner).wait_recv()
    a = ra[:, :, COLS[0] : COLS[0] + AUX].astype(F32)
    tops = a[..., 0:1] + a[..., 1:2] + a[..., 2:3]
    tots = a[..., 3:4] + a[..., 4:5] + a[..., 5:6]
    factor = jnp.exp(tops - jnp.max(tops, axis=0, keepdims=True))
    own_total = jnp.sum(factor * tots, axis=0)
    fb[...] = jnp.broadcast_to(factor, fb.shape)
    own_total = jnp.broadcast_to(own_total, (4, 128))

    def gather_sum(r, k, to):
        cols = pl.ds(k * 128, 128)
        x8[0:4, to : to + 128] = jnp.sum(r[:, :, cols].astype(F32) * fb[...], axis=0) / own_total

    x8[4:8] = jnp.zeros((4, D), F32)
    for i, r in enumerate((ra, rb, rc)):
        if i:
            sum_copy(r, r, i, partner).wait_recv()
        for k in range(COLS[i] // 128):
            gather_sum(r, k, START[i] + k * 128)

    gain_in.wait()
    normed = (x8[...] * gain[...]).astype(BF16)
    win_in.wait()
    wout_in.wait()
    hidden = jax.nn.gelu(jnp.dot(normed, win[...], preferred_element_type=F32)).astype(BF16)

    def row_copy(src, dst, i, target):
        return pltpu.make_async_remote_copy(
            src_ref=src, dst_ref=dst, send_sem=row_send.at[i], recv_sem=row_recv.at[i],
            device_id=target, device_id_type=MESH)

    def show(gs, g, cols, base):
        gs[...] = jnp.dot(hidden, wout[:, cols], preferred_element_type=F32)[0:4].astype(BF16)

        def step(dz, j):
            row_copy(gs, g.at[z, yh, c, x, yl], base + dz, core_of(*chip(dz, j))).start()

        every_chip(step)
        pltpu.make_async_copy(gs, g.at[z, yh, c, x, yl], row_recv.at[base]).start()

    show(gs_a, ga, pl.ds(0, BACK[0]), 0)
    show(gs_b, gb, pl.ds(BACK[0], BACK[1]), 4)
    forwards = {}

    def forward(g, base, dz):
        slab = g.at[(z + 4 - dz) % 4, :, c]
        row_copy(slab, slab, base + dz, partner).wait_recv()
        forwards[base + dz] = pair(slab, slab, 4 + base + dz)
        forwards[base + dz].start()
        copies.append(forwards[base + dz])

    def settle(g, f, base, dz):
        tz = (z + 4 - dz) % 4
        forwards[base + dz].wait_recv()
        f[tz] = g[tz].reshape(128, f.shape[2])
        return tz

    for dz in FAR_FIRST:
        forward(ga, 0, dz)
    for dz in FAR_FIRST:
        settle(ga, fa, 0, dz)
    m_copies = []
    for k in range(BACK[0] // 256):
        cols = pl.ds(k * 256, 256)
        tok[:, cols] = jnp.dot(
            comb[...], fa[:, :, cols].reshape(SLOTS, 256), preferred_element_type=F32).astype(BF16)
        m_copies.append(pltpu.make_async_copy(tok.at[:, cols], mix_out.at[:, cols], out_sem.at[5 + k]))
        m_copies[k].start()
        forward(gb, 4, FAR_FIRST[k])
    forward(gb, 4, FAR_FIRST[3])
    g_copies = []
    for i, dz in enumerate(FAR_FIRST):
        tz = settle(gb, fb_rows, 4, dz)
        g_copies.append(pltpu.make_async_copy(fb_rows.at[tz], g_out.at[tz], out_sem.at[1 + i]))
        g_copies[-1].start()

    for copy in copies:
        copy.wait_send()
    for i, r in enumerate((ra, rb, rc)):
        sent = r.at[pl.ds(0, 63)]
        sum_copy(sent, sent, i, partner).wait_send()
    for base, g, own in ((0, ga, ra.at[pl.ds(0, 30)]), (4, gb, rb.at[pl.ds(0, 15)])):
        slab = g.at[0, :, 0]
        for dz in (1, 2, 3):
            row_copy(slab, slab, base + dz, partner).wait_send()
        row_copy(own, own, base, partner).wait_send()
    comb_copy.wait()
    for copy in g_copies + m_copies:
        copy.wait()


def mix_kernel(comb, rows, first, out, held, sem):
    copies = [pltpu.make_async_copy(first, out.at[:, pl.ds(0, BACK[0])], sem.at[0])]
    copies[0].start()
    half = TOK // 2
    for k, (at, n, col) in enumerate(((0, TOK, 0), (0, half, 256), (half, half, 256))):
        here = (pl.ds(at, n), pl.ds(col, 256))
        held[here] = jnp.dot(comb[pl.ds(at, n)], rows[:, col : col + 256], preferred_element_type=F32).astype(BF16)
        there = out.at[pl.ds(at, n), pl.ds(BACK[0] + col, 256)]
        copies.append(pltpu.make_async_copy(held.at[here], there, sem.at[1 + k]))
        copies[-1].start()
    for copy in copies:
        copy.wait()


def on_device(tokens, slot_keys, norm_gain, w_in, w_out):
    anywhere = pl.BlockSpec(memory_space=pl.ANY)

    def stay(v):
        return pltpu.with_memory_space_constraint(v, pltpu.HBM)

    held = pl.BlockSpec(memory_space=pltpu.VMEM)
    vmem = pltpu.VMEM
    sem = pltpu.SemaphoreType.DMA
    gathered, combine, first = pl.pallas_call(
        kernel,
        out_shape=(
            jax.ShapeDtypeStruct((4, 128, BACK[1]), BF16),
            jax.ShapeDtypeStruct((TOK, SLOTS), BF16),
            jax.ShapeDtypeStruct((TOK, BACK[0]), BF16),
        ),
        in_specs=[anywhere] * 5,
        out_specs=(anywhere,) * 3,
        scratch_shapes=[
            vmem((TOK, D), BF16),
            vmem((D, SLOTS), BF16),
            vmem((TOK, SLOTS), F32),
            vmem((SLOTS, TOK), BF16),
            vmem((TOK, SLOTS), BF16),
            *(vmem((4, 2, 2, 4, 8, n), F32) for n in COLS),
            vmem((1, D), F32),
            vmem((D, FF), BF16),
            vmem((FF, D), BF16),
            vmem((2, 8, SLOTS), F32),
            vmem((4, 2, 2, 4, 8, AUX), F32),
            vmem((64, 4, 128), F32),
            *(vmem((4, 2, 4, 8, n), BF16) for n in COLS),
            *(vmem((4, 2, 4, 8, n), BF16) for n in COLS),
            *(vmem((4, 2, 4, 2, 4, n), BF16) for n in (COLS[0] + AUX, COLS[1], COLS[2])),
            *(vmem((64, 4, n), BF16) for n in (COLS[0] + AUX, COLS[1], COLS[2])),
            vmem((8, D), F32),
            *(vmem((4, n), BF16) for n in BACK),
            *(vmem((4, 2, 2, 4, 2, 4, n), BF16) for n in BACK),
            *(vmem((4, 128, n), BF16) for n in BACK),
            pltpu.SemaphoreType.REGULAR((2,)),
            sem((8,)),
            sem((8,)),
            sem((12,)),
            sem((12,)),
            sem((3,)),
            sem((3,)),
            sem((8,)),
            sem((8,)),
        ],
        compiler_params=pltpu.CompilerParams(
            collective_id=0, has_side_effects=True, vmem_limit_bytes=48 << 20
        ),
        name="route",
    )(*(stay(v) for v in (tokens, slot_keys, norm_gain, w_in, w_out)))
    return pl.pallas_call(
        mix_kernel,
        out_shape=jax.ShapeDtypeStruct((TOK, D), BF16),
        in_specs=[held, held, anywhere],
        out_specs=anywhere,
        scratch_shapes=[vmem((TOK, BACK[1]), BF16), sem((4,))],
        compiler_params=pltpu.CompilerParams(vmem_limit_bytes=12 << 20),
        name="mix",
    )(combine, gathered.reshape(SLOTS, BACK[1]), first)


def solution(mesh):
    return jax.shard_map(
        on_device,
        mesh=mesh,
        in_specs=(
            P(("seq", "grp"), None),
            P(),
            P(("seq", "grp"), None),
            P(("seq", "grp"), None, None),
            P(("seq", "grp"), None, None),
        ),
        out_specs=P(("seq", "grp"), None),
        check_vma=False,
    )
```

```python
import jax
import jax.numpy as jnp
from jax import lax
from jax.experimental import pallas as pl
from jax.experimental.pallas import tpu as pltpu
from jax.sharding import PartitionSpec as P

F32 = jnp.float32
BF16 = jnp.bfloat16
MESH = pl.DeviceIdType.MESH
TOK, D, FF, SLOTS = 2048, 1280, 2560, 512
LOADS = (256, 256, 512, 1024)
TILE = 512
COLS = (512, 768)
START = (0, 512)
AUX = 128
FAR_FIRST = (2, 1, 3, 0)


def place():
    seq = lax.axis_index("seq")
    grp = lax.axis_index("grp")
    return seq // 4, (seq // 2) % 2, seq % 2, grp // 2, grp % 2


def split3(v):
    hi = v.astype(BF16).astype(F32)
    mid = (v - hi).astype(BF16).astype(F32)
    lo = (v - hi - mid).astype(BF16).astype(F32)
    return hi, mid, lo


def kernel(tok_h, key_h, gain_h, win_h, wout_h, g_out, comb_out,
           tok, key, logit, sct, comb, numer_a, numer_b, gain, win, wout, aux, fcol, fb,
           csend_a, csend_b, crecv_a, crecv_b, sa, sb, ra, rb, x8, gs, g, gf,
           in_sem, load_sem, out_sem, pair_out, pair_in, sum_send, sum_recv, row_send, row_recv):
    z, yh, c, x, yl = place()
    y = yh * 2 + yl
    partner = ((z * 2 + yh) * 2 + 1 - c, x * 2 + yl)

    key_in = pltpu.make_async_copy(key_h, key, load_sem.at[7])
    key_in.start()
    tok_in, at = [], 0
    for i, n in enumerate(LOADS):
        rows = pl.ds(at, n)
        tok_in.append(pltpu.make_async_copy(tok_h.at[rows], tok.at[rows], load_sem.at[i]))
        tok_in[-1].start()
        at += n
    gain_in = pltpu.make_async_copy(gain_h, gain, load_sem.at[6])
    win_in = pltpu.make_async_copy(win_h.at[0], win, load_sem.at[4])
    wout_in = pltpu.make_async_copy(wout_h.at[0], wout, load_sem.at[5])

    def chip(dz, j):
        tz, ty, tx = (z + dz) % 4, (y + j // 4) % 4, (x + j % 4) % 4
        return tz, ty // 2, tx, ty % 2

    def core_of(tz, tyh, tx, tyl):
        return (tz * 2 + tyh) * 2 + c, tx * 2 + tyl

    def every_chip(act, steps=FAR_FIRST):
        for dz in steps:
            def step(j, carry, dz=dz):
                act(dz, j)
                return carry
            lax.fori_loop(0 if dz else 1, 16, step, 0)

    barrier = pltpu.get_barrier_semaphore()
    pl.semaphore_signal(barrier, inc=1, device_id=partner, device_id_type=MESH)

    def line(axis, d):
        if axis == "x":
            return core_of(z, yh, (x + d) % 4, yl)
        if axis == "y":
            ty = (y + d) % 4
            return core_of(z, ty // 2, x, ty % 2)
        return core_of((z + d) % 4, yh, x, yl)

    def greet(sem, axes):
        for axis in axes:
            for d in (1, 2, 3):
                pl.semaphore_signal(sem, inc=1, device_id=line(axis, d), device_id_type=MESH)

    greet(barrier, "xyz")

    def pair(src, dst, i):
        return pltpu.make_async_remote_copy(
            src_ref=src, dst_ref=dst, send_sem=pair_out.at[i], recv_sem=pair_in.at[i],
            device_id=partner, device_id_type=MESH)

    key_in.wait()
    peak8 = jnp.full((8, SLOTS), -jnp.inf, F32)
    at = 0
    for i, n in enumerate(LOADS):
        rows = pl.ds(at, n)
        tok_in[i].wait()
        part = jnp.dot(tok[rows], key[...], preferred_element_type=F32)
        logit[rows] = part
        peak8 = jnp.maximum(peak8, jnp.max(part.reshape(n // 8, 8, SLOTS), axis=0))
        at += n
        if i == 1:
            pl.semaphore_wait(barrier, 10)
            greet(in_sem.at[0], "y")
        if i == 2:
            pl.semaphore_wait(in_sem.at[0], 3)
            greet(in_sem.at[1], "z")
    win_in.start()
    wout_in.start()
    gain_in.start()
    peak = jnp.max(peak8, axis=0, keepdims=True)

    def score_step(t, total8):
        rows = pl.ds(pl.multiple_of(t * TILE, TILE), TILE)
        scores = jnp.exp(logit[rows] - peak)
        sct[:, rows] = scores.astype(BF16).T
        return total8 + jnp.sum(scores.reshape(TILE // 8, 8, SLOTS), axis=0)

    total8 = lax.fori_loop(0, TOK // TILE, score_step, jnp.zeros((8, SLOTS), F32))
    total = jnp.sum(total8, axis=0, keepdims=True)
    row = lax.broadcasted_iota(jnp.int32, (8, SLOTS), 0)
    aux[0] = jnp.where(row == 0, peak, jnp.where(row == 1, total, 0.0))
    copies = [pair(aux.at[0], aux.at[1], 0)]
    copies[0].start()

    def numer_part(at, n, numer, to):
        part = jnp.dot(sct[...], tok[:, at : at + n], preferred_element_type=F32)
        numer[..., to : to + n] = part.reshape(4, 2, 2, 4, 8, n)

    def pair_send(numer, csend, crecv, i):
        csend[...] = numer[:, :, 1 - c].astype(BF16)
        copies.append(pair(csend, crecv, i))
        copies[i].start()

    numer_part(0, COLS[0], numer_a, 0)
    pair_send(numer_a, csend_a, crecv_a, 1)

    copies[0].wait_recv()
    tops, tots = (peak, aux[1][0:1]), (total, aux[1][1:2])
    top = jnp.maximum(*tops)
    factors = [jnp.exp(p - top) for p in tops]
    tot = factors[0] * tots[0] + factors[1] * tots[1]
    line = lax.broadcasted_iota(jnp.int32, (AUX, SLOTS), 0)
    block = jnp.zeros((AUX, SLOTS), F32)
    for i, v in enumerate(split3(top) + split3(tot) + tuple(factors)):
        block = jnp.where(line == i, v, block)
    fcol[...] = block.T.reshape(4, 2, 2, 4, 8, AUX)

    def sum_copy(src, dst, i, target):
        return pltpu.make_async_remote_copy(
            src_ref=src, dst_ref=dst, send_sem=sum_send.at[i], recv_sem=sum_recv.at[i],
            device_id=target, device_id_type=MESH)

    def pair_sum(numer, crecv, s, i, n):
        copies[i].wait_recv()

        def step(tz, carry):
            f = fcol[tz, :, c]
            both = numer[tz, :, c] * f[..., 6:7] + crecv[tz].astype(F32) * f[..., 7:8]
            for h in range(2):
                s[tz, :, :, h, :, 0:n] = both[:, :, 4 * h : 4 * h + 4].astype(BF16)
                if i == 1:
                    s[tz, :, :, h, :, n : n + AUX] = f[:, :, 4 * h : 4 * h + 4].astype(BF16)
            return carry

        lax.fori_loop(0, 4, step, 0)

    def give(s, r, i, steps):
        def step(dz, j):
            to = chip(dz, j)
            sum_copy(s.at[to], r.at[dz * 16 + j], i - 1, core_of(*to)).start()

        every_chip(step, steps)
        if 0 in steps:
            pltpu.make_async_copy(s.at[z, yh, x, yl], r.at[0], sum_recv.at[i - 1]).start()

    numer_part(512, 256, numer_b, 0)
    pl.semaphore_wait(in_sem.at[1], 3)
    pair_sum(numer_a, crecv_a, sa, 1, COLS[0])
    give(sa, ra, 1, (2,))
    numer_part(768, 256, numer_b, 256)
    give(sa, ra, 1, (1,))
    numer_part(1024, 256, numer_b, 512)
    pair_send(numer_b, csend_b, crecv_b, 2)
    give(sa, ra, 1, (3, 0))
    pair_sum(numer_b, crecv_b, sb, 2, COLS[1])
    give(sb, rb, 2, FAR_FIRST)

    def combine_step(t, carry):
        rows = pl.ds(pl.multiple_of(t * 256, 256), 256)
        e = logit[rows]
        e = jnp.exp(e - jnp.max(e, axis=1, keepdims=True))
        comb[rows] = (e / jnp.sum(e, axis=1, keepdims=True)).astype(BF16)
        return carry

    lax.fori_loop(0, TOK // 256, combine_step, 0)
    comb_copy = pltpu.make_async_copy(comb, comb_out, out_sem.at[0])
    comb_copy.start()

    sum_copy(ra, ra, 0, partner).wait_recv()
    a = ra[:, :, COLS[0] : COLS[0] + AUX].astype(F32)
    tops = a[..., 0:1] + a[..., 1:2] + a[..., 2:3]
    tots = a[..., 3:4] + a[..., 4:5] + a[..., 5:6]
    factor = jnp.exp(tops - jnp.max(tops, axis=0, keepdims=True))
    own_total = jnp.sum(factor * tots, axis=0)
    fb[...] = jnp.broadcast_to(factor, fb.shape)
    own_total = jnp.broadcast_to(own_total, (4, 128))

    def gather_sum(r, k, to):
        cols = pl.ds(k * 128, 128)
        x8[0:4, to : to + 128] = jnp.sum(r[:, :, cols].astype(F32) * fb[...], axis=0) / own_total

    x8[4:8] = jnp.zeros((4, D), F32)
    for i, r in enumerate((ra, rb)):
        if i:
            sum_copy(r, r, i, partner).wait_recv()
        for k in range(COLS[i] // 128):
            gather_sum(r, k, START[i] + k * 128)

    gain_in.wait()
    normed = (x8[...] * gain[...]).astype(BF16)
    win_in.wait()
    wout_in.wait()
    hidden = jax.nn.gelu(jnp.dot(normed, win[...], preferred_element_type=F32)).astype(BF16)
    gs[...] = jnp.dot(hidden, wout[...], preferred_element_type=F32)[0:4].astype(BF16)

    def row_copy(src, dst, i, target):
        return pltpu.make_async_remote_copy(
            src_ref=src, dst_ref=dst, send_sem=row_send.at[i], recv_sem=row_recv.at[i],
            device_id=target, device_id_type=MESH)

    def show(dz, j):
        row_copy(gs, g.at[z, yh, c, x, yl], dz, core_of(*chip(dz, j))).start()

    every_chip(show)
    pltpu.make_async_copy(gs, g.at[z, yh, c, x, yl], row_recv.at[0]).start()
    for dz in FAR_FIRST:
        slab = g.at[(z + 4 - dz) % 4, :, c]
        row_copy(slab, slab, dz, partner).wait_recv()
        copies.append(pair(slab, slab, 3 + dz))
        copies[-1].start()
    g_copies = []
    for i, dz in enumerate(FAR_FIRST):
        tz = (z + 4 - dz) % 4
        copies[3 + i].wait_recv()
        gf[tz] = g[tz].reshape(128, D)
        g_copies.append(pltpu.make_async_copy(gf.at[tz], g_out.at[tz], out_sem.at[1 + i]))
        g_copies[-1].start()

    for copy in copies:
        copy.wait_send()
    for i, r in enumerate((ra, rb)):
        sent = r.at[pl.ds(0, 63)]
        sum_copy(sent, sent, i, partner).wait_send()
    slab = g.at[0, :, 0]
    for dz in (1, 2, 3):
        row_copy(slab, slab, dz, partner).wait_send()
    part = ra.at[pl.ds(0, 30)]
    row_copy(part, part, 0, partner).wait_send()
    comb_copy.wait()
    for copy in g_copies:
        copy.wait()


def mix_kernel(comb, rows, out, held, sem):
    copies = []
    for k, (at, n) in enumerate(((0, TOK), (0, TOK), (0, TOK), (0, TOK), (0, TOK // 2), (TOK // 2, TOK // 2))):
        block = (pl.ds(at, n), pl.ds(min(k, 4) * 256, 256))
        held[block] = jnp.dot(comb[block[0]], rows[:, block[1]], preferred_element_type=F32).astype(BF16)
        copies.append(pltpu.make_async_copy(held.at[block], out.at[block], sem.at[k]))
        copies[k].start()
    for copy in copies:
        copy.wait()


def on_device(tokens, slot_keys, norm_gain, w_in, w_out):
    anywhere = pl.BlockSpec(memory_space=pl.ANY)

    def stay(v):
        return pltpu.with_memory_space_constraint(v, pltpu.HBM)

    held = pl.BlockSpec(memory_space=pltpu.VMEM)
    vmem = pltpu.VMEM
    sem = pltpu.SemaphoreType.DMA
    gathered, combine = pl.pallas_call(
        kernel,
        out_shape=(
            jax.ShapeDtypeStruct((4, 128, D), BF16),
            jax.ShapeDtypeStruct((TOK, SLOTS), BF16),
        ),
        in_specs=[anywhere] * 5,
        out_specs=(anywhere, anywhere),
        scratch_shapes=[
            vmem((TOK, D), BF16),
            vmem((D, SLOTS), BF16),
            vmem((TOK, SLOTS), F32),
            vmem((SLOTS, TOK), BF16),
            vmem((TOK, SLOTS), BF16),
            *(vmem((4, 2, 2, 4, 8, n), F32) for n in COLS),
            vmem((1, D), F32),
            vmem((D, FF), BF16),
            vmem((FF, D), BF16),
            vmem((2, 8, SLOTS), F32),
            vmem((4, 2, 2, 4, 8, AUX), F32),
            vmem((64, 4, 128), F32),
            *(vmem((4, 2, 4, 8, n), BF16) for n in COLS),
            *(vmem((4, 2, 4, 8, n), BF16) for n in COLS),
            *(vmem((4, 2, 4, 2, 4, n), BF16) for n in (COLS[0] + AUX, COLS[1])),
            *(vmem((64, 4, n), BF16) for n in (COLS[0] + AUX, COLS[1])),
            vmem((8, D), F32),
            vmem((4, D), BF16),
            vmem((4, 2, 2, 4, 2, 4, D), BF16),
            vmem((4, 128, D), BF16),
            pltpu.SemaphoreType.REGULAR((2,)),
            sem((8,)),
            sem((5,)),
            sem((7,)),
            sem((7,)),
            sem((2,)),
            sem((2,)),
            sem((4,)),
            sem((4,)),
        ],
        compiler_params=pltpu.CompilerParams(
            collective_id=0, has_side_effects=True, vmem_limit_bytes=48 << 20
        ),
        name="route",
    )(*(stay(v) for v in (tokens, slot_keys, norm_gain, w_in, w_out)))
    return pl.pallas_call(
        mix_kernel,
        out_shape=jax.ShapeDtypeStruct((TOK, D), BF16),
        in_specs=[held, held],
        out_specs=anywhere,
        scratch_shapes=[vmem((TOK, D), BF16), sem((6,))],
        compiler_params=pltpu.CompilerParams(vmem_limit_bytes=12 << 20),
        name="mix",
    )(combine, gathered.reshape(SLOTS, D))


def solution(mesh):
    return jax.shard_map(
        on_device,
        mesh=mesh,
        in_specs=(
            P(("seq", "grp"), None),
            P(),
            P(("seq", "grp"), None),
            P(("seq", "grp"), None, None),
            P(("seq", "grp"), None, None),
        ),
        out_specs=P(("seq", "grp"), None),
        check_vma=False,
    )
```

```python
import jax
import jax.numpy as jnp
from jax import lax
from jax.experimental import pallas as pl
from jax.experimental.pallas import tpu as pltpu
from jax.sharding import PartitionSpec as P

F32 = jnp.float32
BF16 = jnp.bfloat16
MESH = pl.DeviceIdType.MESH
TOK, D, FF, SLOTS = 2048, 1280, 2560, 512
LOADS = (256, 256, 512, 1024)
TILE = 512
COLS = (512, 768)
START = (0, 512)
AUX = 128
FAR_FIRST = (2, 1, 3, 0)


def place():
    seq = lax.axis_index("seq")
    grp = lax.axis_index("grp")
    return seq // 4, (seq // 2) % 2, seq % 2, grp // 2, grp % 2


def split3(v):
    hi = v.astype(BF16).astype(F32)
    mid = (v - hi).astype(BF16).astype(F32)
    lo = (v - hi - mid).astype(BF16).astype(F32)
    return hi, mid, lo


def kernel(tok_h, key_h, gain_h, win_h, wout_h, g_out, comb_out,
           tok, key, logit, sct, comb, numer_a, numer_b, gain, win, wout, aux, fcol, fb,
           csend_a, csend_b, crecv_a, crecv_b, sa, sb, ra, rb, x8, gs, g, gf,
           in_sem, load_sem, out_sem, pair_out, pair_in, sum_send, sum_recv, row_send, row_recv):
    z, yh, c, x, yl = place()
    y = yh * 2 + yl
    partner = ((z * 2 + yh) * 2 + 1 - c, x * 2 + yl)

    key_in = pltpu.make_async_copy(key_h, key, load_sem.at[7])
    key_in.start()
    tok_in, at = [], 0
    for i, n in enumerate(LOADS):
        rows = pl.ds(at, n)
        tok_in.append(pltpu.make_async_copy(tok_h.at[rows], tok.at[rows], load_sem.at[i]))
        tok_in[-1].start()
        at += n
    gain_in = pltpu.make_async_copy(gain_h, gain, load_sem.at[6])
    win_in = pltpu.make_async_copy(win_h.at[0], win, load_sem.at[4])
    wout_in = pltpu.make_async_copy(wout_h.at[0], wout, load_sem.at[5])

    zs = [lax.rem(z + d, 4) for d in range(4)]
    xs = [lax.rem(x + d, 4) for d in range(4)]
    z_part = [tz * 4 + c for tz in zs]
    x_part = [tx * 2 for tx in xs]

    def core_of(tz, tyh, tx, tyl):
        return (tz * 2 + tyh) * 2 + c, tx * 2 + tyl

    def every_chip(act, steps=FAR_FIRST):
        for dz in steps:
            def along(dy, carry, dz=dz, first=0):
                ty = lax.rem(y + dy, 4)
                tyh, tyl = lax.div(ty, 2), lax.rem(ty, 2)
                for dx in range(first, 4):
                    device = (z_part[dz] + tyh * 2, x_part[dx] + tyl)
                    act((zs[dz], tyh, xs[dx], tyl), dz * 16 + dy * 4 + dx, device)
                return carry
            if dz == 0:
                along(0, 0, first=1)
            lax.fori_loop(0 if dz else 1, 4, along, 0)

    barrier = pltpu.get_barrier_semaphore()
    pl.semaphore_signal(barrier, inc=1, device_id=partner, device_id_type=MESH)

    def line(axis, d):
        if axis == "x":
            return core_of(z, yh, (x + d) % 4, yl)
        if axis == "y":
            ty = (y + d) % 4
            return core_of(z, ty // 2, x, ty % 2)
        return core_of((z + d) % 4, yh, x, yl)

    def greet(sem, axes):
        for axis in axes:
            for d in (1, 2, 3):
                pl.semaphore_signal(sem, inc=1, device_id=line(axis, d), device_id_type=MESH)

    greet(barrier, "xyz")

    def pair(src, dst, i):
        return pltpu.make_async_remote_copy(
            src_ref=src, dst_ref=dst, send_sem=pair_out.at[i], recv_sem=pair_in.at[i],
            device_id=partner, device_id_type=MESH)

    key_in.wait()
    peak8 = jnp.full((8, SLOTS), -jnp.inf, F32)
    at = 0
    for i, n in enumerate(LOADS):
        rows = pl.ds(at, n)
        tok_in[i].wait()
        part = jnp.dot(tok[rows], key[...], preferred_element_type=F32)
        logit[rows] = part
        peak8 = jnp.maximum(peak8, jnp.max(part.reshape(n // 8, 8, SLOTS), axis=0))
        at += n
        if i == 1:
            pl.semaphore_wait(barrier, 10)
            greet(in_sem.at[0], "y")
        if i == 2:
            pl.semaphore_wait(in_sem.at[0], 3)
            greet(in_sem.at[1], "z")
    win_in.start()
    wout_in.start()
    gain_in.start()
    peak = jnp.max(peak8, axis=0, keepdims=True)

    def score_step(t, total8):
        rows = pl.ds(pl.multiple_of(t * TILE, TILE), TILE)
        scores = jnp.exp(logit[rows] - peak)
        sct[:, rows] = scores.astype(BF16).T
        return total8 + jnp.sum(scores.reshape(TILE // 8, 8, SLOTS), axis=0)

    total8 = lax.fori_loop(0, TOK // TILE, score_step, jnp.zeros((8, SLOTS), F32))
    total = jnp.sum(total8, axis=0, keepdims=True)
    row = lax.broadcasted_iota(jnp.int32, (8, SLOTS), 0)
    aux[0] = jnp.where(row == 0, peak, jnp.where(row == 1, total, 0.0))
    copies = [pair(aux.at[0], aux.at[1], 0)]
    copies[0].start()

    def numer_part(at, n, numer, to):
        part = jnp.dot(sct[...], tok[:, at : at + n], preferred_element_type=F32)
        numer[..., to : to + n] = part.reshape(4, 2, 2, 4, 8, n)

    def pair_send(numer, csend, crecv, i):
        csend[...] = numer[:, :, 1 - c].astype(BF16)
        copies.append(pair(csend, crecv, i))
        copies[i].start()

    numer_part(0, COLS[0], numer_a, 0)
    pair_send(numer_a, csend_a, crecv_a, 1)

    copies[0].wait_recv()
    tops, tots = (peak, aux[1][0:1]), (total, aux[1][1:2])
    top = jnp.maximum(*tops)
    factors = [jnp.exp(p - top) for p in tops]
    tot = factors[0] * tots[0] + factors[1] * tots[1]
    line = lax.broadcasted_iota(jnp.int32, (AUX, SLOTS), 0)
    block = jnp.zeros((AUX, SLOTS), F32)
    for i, v in enumerate(split3(top) + split3(tot) + tuple(factors)):
        block = jnp.where(line == i, v, block)
    fcol[...] = block.T.reshape(4, 2, 2, 4, 8, AUX)

    def sum_copy(src, dst, i, target):
        return pltpu.make_async_remote_copy(
            src_ref=src, dst_ref=dst, send_sem=sum_send.at[i], recv_sem=sum_recv.at[i],
            device_id=target, device_id_type=MESH)

    def pair_sum(numer, crecv, s, i, n):
        copies[i].wait_recv()

        def step(tz, carry):
            f = fcol[tz, :, c]
            both = numer[tz, :, c] * f[..., 6:7] + crecv[tz].astype(F32) * f[..., 7:8]
            for h in range(2):
                s[tz, :, :, h, :, 0:n] = both[:, :, 4 * h : 4 * h + 4].astype(BF16)
                if i == 1:
                    s[tz, :, :, h, :, n : n + AUX] = f[:, :, 4 * h : 4 * h + 4].astype(BF16)
            return carry

        lax.fori_loop(0, 4, step, 0)

    def give(s, r, i, steps):
        def step(to, number, device):
            sum_copy(s.at[to], r.at[number], i - 1, device).start()

        every_chip(step, steps)
        if 0 in steps:
            pltpu.make_async_copy(s.at[z, yh, x, yl], r.at[0], sum_recv.at[i - 1]).start()

    numer_part(512, 256, numer_b, 0)
    pl.semaphore_wait(in_sem.at[1], 3)
    pair_sum(numer_a, crecv_a, sa, 1, COLS[0])
    give(sa, ra, 1, (2,))
    numer_part(768, 256, numer_b, 256)
    give(sa, ra, 1, (1,))
    numer_part(1024, 256, numer_b, 512)
    pair_send(numer_b, csend_b, crecv_b, 2)
    give(sa, ra, 1, (3, 0))
    pair_sum(numer_b, crecv_b, sb, 2, COLS[1])
    give(sb, rb, 2, FAR_FIRST)

    def combine_step(t, carry):
        rows = pl.ds(pl.multiple_of(t * 256, 256), 256)
        e = logit[rows]
        e = jnp.exp(e - jnp.max(e, axis=1, keepdims=True))
        comb[rows] = (e / jnp.sum(e, axis=1, keepdims=True)).astype(BF16)
        return carry

    lax.fori_loop(0, TOK // 256, combine_step, 0)
    comb_copy = pltpu.make_async_copy(comb, comb_out, out_sem.at[0])
    comb_copy.start()

    sum_copy(ra, ra, 0, partner).wait_recv()
    a = ra[:, :, COLS[0] : COLS[0] + AUX].astype(F32)
    tops = a[..., 0:1] + a[..., 1:2] + a[..., 2:3]
    tots = a[..., 3:4] + a[..., 4:5] + a[..., 5:6]
    factor = jnp.exp(tops - jnp.max(tops, axis=0, keepdims=True))
    own_total = jnp.sum(factor * tots, axis=0)
    fb[...] = jnp.broadcast_to(factor, fb.shape)
    own_total = jnp.broadcast_to(own_total, (4, 128))

    def gather_sum(r, k, to):
        cols = pl.ds(k * 128, 128)
        x8[0:4, to : to + 128] = jnp.sum(r[:, :, cols].astype(F32) * fb[...], axis=0) / own_total

    x8[4:8] = jnp.zeros((4, D), F32)
    for i, r in enumerate((ra, rb)):
        if i:
            sum_copy(r, r, i, partner).wait_recv()
        for k in range(COLS[i] // 128):
            gather_sum(r, k, START[i] + k * 128)

    gain_in.wait()
    normed = (x8[...] * gain[...]).astype(BF16)
    win_in.wait()
    wout_in.wait()
    hidden = jax.nn.gelu(jnp.dot(normed, win[...], preferred_element_type=F32)).astype(BF16)
    gs[...] = jnp.dot(hidden, wout[...], preferred_element_type=F32)[0:4].astype(BF16)

    def row_copy(src, dst, i, target):
        return pltpu.make_async_remote_copy(
            src_ref=src, dst_ref=dst, send_sem=row_send.at[i], recv_sem=row_recv.at[i],
            device_id=target, device_id_type=MESH)

    for dz in FAR_FIRST:
        def show(to, number, device, dz=dz):
            row_copy(gs, g.at[z, yh, c, x, yl], dz, device).start()

        every_chip(show, (dz,))
    pltpu.make_async_copy(gs, g.at[z, yh, c, x, yl], row_recv.at[0]).start()
    for dz in FAR_FIRST:
        slab = g.at[(z + 4 - dz) % 4, :, c]
        row_copy(slab, slab, dz, partner).wait_recv()
        copies.append(pair(slab, slab, 3 + dz))
        copies[-1].start()
    g_copies = []
    for i, dz in enumerate(FAR_FIRST):
        tz = (z + 4 - dz) % 4
        copies[3 + i].wait_recv()
        gf[tz] = g[tz].reshape(128, D)
        g_copies.append(pltpu.make_async_copy(gf.at[tz], g_out.at[tz], out_sem.at[1 + i]))
        g_copies[-1].start()

    for copy in copies:
        copy.wait_send()
    for i, r in enumerate((ra, rb)):
        sent = r.at[pl.ds(0, 63)]
        sum_copy(sent, sent, i, partner).wait_send()
    slab = g.at[0, :, 0]
    for dz in (1, 2, 3):
        row_copy(slab, slab, dz, partner).wait_send()
    part = ra.at[pl.ds(0, 30)]
    row_copy(part, part, 0, partner).wait_send()
    comb_copy.wait()
    for copy in g_copies:
        copy.wait()


def mix_kernel(comb, rows, out, held, sem):
    copies = []
    for k, (at, n) in enumerate(((0, TOK), (0, TOK), (0, TOK), (0, TOK), (0, TOK // 2), (TOK // 2, TOK // 2))):
        block = (pl.ds(at, n), pl.ds(min(k, 4) * 256, 256))
        held[block] = jnp.dot(comb[block[0]], rows[:, block[1]], preferred_element_type=F32).astype(BF16)
        copies.append(pltpu.make_async_copy(held.at[block], out.at[block], sem.at[k]))
        copies[k].start()
    for copy in copies:
        copy.wait()


def on_device(tokens, slot_keys, norm_gain, w_in, w_out):
    anywhere = pl.BlockSpec(memory_space=pl.ANY)

    def stay(v):
        return pltpu.with_memory_space_constraint(v, pltpu.HBM)

    held = pl.BlockSpec(memory_space=pltpu.VMEM)
    vmem = pltpu.VMEM
    sem = pltpu.SemaphoreType.DMA
    gathered, combine = pl.pallas_call(
        kernel,
        out_shape=(
            jax.ShapeDtypeStruct((4, 128, D), BF16),
            jax.ShapeDtypeStruct((TOK, SLOTS), BF16),
        ),
        in_specs=[anywhere] * 5,
        out_specs=(anywhere, anywhere),
        scratch_shapes=[
            vmem((TOK, D), BF16),
            vmem((D, SLOTS), BF16),
            vmem((TOK, SLOTS), F32),
            vmem((SLOTS, TOK), BF16),
            vmem((TOK, SLOTS), BF16),
            *(vmem((4, 2, 2, 4, 8, n), F32) for n in COLS),
            vmem((1, D), F32),
            vmem((D, FF), BF16),
            vmem((FF, D), BF16),
            vmem((2, 8, SLOTS), F32),
            vmem((4, 2, 2, 4, 8, AUX), F32),
            vmem((64, 4, 128), F32),
            *(vmem((4, 2, 4, 8, n), BF16) for n in COLS),
            *(vmem((4, 2, 4, 8, n), BF16) for n in COLS),
            *(vmem((4, 2, 4, 2, 4, n), BF16) for n in (COLS[0] + AUX, COLS[1])),
            *(vmem((64, 4, n), BF16) for n in (COLS[0] + AUX, COLS[1])),
            vmem((8, D), F32),
            vmem((4, D), BF16),
            vmem((4, 2, 2, 4, 2, 4, D), BF16),
            vmem((4, 128, D), BF16),
            pltpu.SemaphoreType.REGULAR((2,)),
            sem((8,)),
            sem((5,)),
            sem((7,)),
            sem((7,)),
            sem((2,)),
            sem((2,)),
            sem((4,)),
            sem((4,)),
        ],
        compiler_params=pltpu.CompilerParams(
            collective_id=0, has_side_effects=True, vmem_limit_bytes=48 << 20
        ),
        name="route",
    )(*(stay(v) for v in (tokens, slot_keys, norm_gain, w_in, w_out)))
    return pl.pallas_call(
        mix_kernel,
        out_shape=jax.ShapeDtypeStruct((TOK, D), BF16),
        in_specs=[held, held],
        out_specs=anywhere,
        scratch_shapes=[vmem((TOK, D), BF16), sem((6,))],
        compiler_params=pltpu.CompilerParams(vmem_limit_bytes=12 << 20),
        name="mix",
    )(combine, gathered.reshape(SLOTS, D))


def solution(mesh):
    return jax.shard_map(
        on_device,
        mesh=mesh,
        in_specs=(
            P(("seq", "grp"), None),
            P(),
            P(("seq", "grp"), None),
            P(("seq", "grp"), None, None),
            P(("seq", "grp"), None, None),
        ),
        out_specs=P(("seq", "grp"), None),
        check_vma=False,
    )
```

```python
import jax
import jax.numpy as jnp
from jax import lax
from jax.experimental import pallas as pl
from jax.experimental.pallas import tpu as pltpu
from jax.sharding import PartitionSpec as P

F32 = jnp.float32
BF16 = jnp.bfloat16
MESH = pl.DeviceIdType.MESH
TOK, D, FF, SLOTS = 2048, 1280, 2560, 512
LOADS = (256, 256, 512, 1024)
TILE = 512
COLS = (512, 768)
START = (0, 512)
AUX = 128
FAR_FIRST = (2, 1, 3, 0)


def place():
    seq = lax.axis_index("seq")
    grp = lax.axis_index("grp")
    return seq // 4, (seq // 2) % 2, seq % 2, grp // 2, grp % 2


def split3(v):
    hi = v.astype(BF16).astype(F32)
    mid = (v - hi).astype(BF16).astype(F32)
    lo = (v - hi - mid).astype(BF16).astype(F32)
    return hi, mid, lo


def kernel(tok_h, key_h, gain_h, win_h, wout_h, gf, comb_out,
           tok, key, logit, sct, comb, numer_a, numer_b, gain, win, wout, aux, fcol, fb,
           csend_a, csend_b, crecv_a, crecv_b, sa, sb, ra, rb, x8, gs, g,
           in_sem, load_sem, out_sem, pair_out, pair_in, sum_send, sum_recv, row_send, row_recv):
    z, yh, c, x, yl = place()
    y = yh * 2 + yl
    partner = ((z * 2 + yh) * 2 + 1 - c, x * 2 + yl)

    key_in = pltpu.make_async_copy(key_h, key, load_sem.at[7])
    key_in.start()
    tok_in, at = [], 0
    for i, n in enumerate(LOADS):
        rows = pl.ds(at, n)
        tok_in.append(pltpu.make_async_copy(tok_h.at[rows], tok.at[rows], load_sem.at[i]))
        tok_in[-1].start()
        at += n
    gain_in = pltpu.make_async_copy(gain_h, gain, load_sem.at[6])
    win_in = pltpu.make_async_copy(win_h.at[0], win, load_sem.at[4])
    wout_in = pltpu.make_async_copy(wout_h.at[0], wout, load_sem.at[5])

    zs = [lax.rem(z + d, 4) for d in range(4)]
    xs = [lax.rem(x + d, 4) for d in range(4)]
    z_part = [tz * 4 + c for tz in zs]
    x_part = [tx * 2 for tx in xs]

    def core_of(tz, tyh, tx, tyl):
        return (tz * 2 + tyh) * 2 + c, tx * 2 + tyl

    def every_chip(act, steps=FAR_FIRST):
        for dz in steps:
            def along(dy, carry, dz=dz, first=0):
                ty = lax.rem(y + dy, 4)
                tyh, tyl = lax.div(ty, 2), lax.rem(ty, 2)
                for dx in range(first, 4):
                    device = (z_part[dz] + tyh * 2, x_part[dx] + tyl)
                    act((zs[dz], tyh, xs[dx], tyl), dz * 16 + dy * 4 + dx, device)
                return carry
            if dz == 0:
                along(0, 0, first=1)
            lax.fori_loop(0 if dz else 1, 4, along, 0)

    barrier = pltpu.get_barrier_semaphore()
    pl.semaphore_signal(barrier, inc=1, device_id=partner, device_id_type=MESH)

    def line(axis, d):
        if axis == "x":
            return core_of(z, yh, (x + d) % 4, yl)
        if axis == "y":
            ty = (y + d) % 4
            return core_of(z, ty // 2, x, ty % 2)
        return core_of((z + d) % 4, yh, x, yl)

    def greet(sem, axes):
        for axis in axes:
            for d in (1, 2, 3):
                pl.semaphore_signal(sem, inc=1, device_id=line(axis, d), device_id_type=MESH)

    greet(barrier, "xyz")

    def pair(src, dst, i):
        return pltpu.make_async_remote_copy(
            src_ref=src, dst_ref=dst, send_sem=pair_out.at[i], recv_sem=pair_in.at[i],
            device_id=partner, device_id_type=MESH)

    key_in.wait()
    peak8 = jnp.full((8, SLOTS), -jnp.inf, F32)
    at = 0
    for i, n in enumerate(LOADS):
        rows = pl.ds(at, n)
        tok_in[i].wait()
        part = jnp.dot(tok[rows], key[...], preferred_element_type=F32)
        logit[rows] = part
        peak8 = jnp.maximum(peak8, jnp.max(part.reshape(n // 8, 8, SLOTS), axis=0))
        at += n
        if i == 1:
            pl.semaphore_wait(barrier, 10)
            greet(in_sem.at[0], "y")
        if i == 2:
            pl.semaphore_wait(in_sem.at[0], 3)
            greet(in_sem.at[1], "z")
    win_in.start()
    wout_in.start()
    gain_in.start()
    peak = jnp.max(peak8, axis=0, keepdims=True)

    def score_step(t, total8):
        rows = pl.ds(pl.multiple_of(t * TILE, TILE), TILE)
        scores = jnp.exp(logit[rows] - peak)
        sct[:, rows] = scores.astype(BF16).T
        return total8 + jnp.sum(scores.reshape(TILE // 8, 8, SLOTS), axis=0)

    total8 = lax.fori_loop(0, TOK // TILE, score_step, jnp.zeros((8, SLOTS), F32))
    total = jnp.sum(total8, axis=0, keepdims=True)
    row = lax.broadcasted_iota(jnp.int32, (8, SLOTS), 0)
    aux[0] = jnp.where(row == 0, peak, jnp.where(row == 1, total, 0.0))
    copies = [pair(aux.at[0], aux.at[1], 0)]
    copies[0].start()

    def numer_part(at, n, numer, to):
        part = jnp.dot(sct[...], tok[:, at : at + n], preferred_element_type=F32)
        numer[..., to : to + n] = part.reshape(4, 2, 2, 4, 8, n)

    def pair_send(numer, csend, crecv, i):
        csend[...] = numer[:, :, 1 - c].astype(BF16)
        copies.append(pair(csend, crecv, i))
        copies[i].start()

    numer_part(0, COLS[0], numer_a, 0)
    pair_send(numer_a, csend_a, crecv_a, 1)

    copies[0].wait_recv()
    tops, tots = (peak, aux[1][0:1]), (total, aux[1][1:2])
    top = jnp.maximum(*tops)
    factors = [jnp.exp(p - top) for p in tops]
    tot = factors[0] * tots[0] + factors[1] * tots[1]
    line = lax.broadcasted_iota(jnp.int32, (AUX, SLOTS), 0)
    block = jnp.zeros((AUX, SLOTS), F32)
    for i, v in enumerate(split3(top) + split3(tot) + tuple(factors)):
        block = jnp.where(line == i, v, block)
    fcol[...] = block.T.reshape(4, 2, 2, 4, 8, AUX)

    def sum_copy(src, dst, i, target):
        return pltpu.make_async_remote_copy(
            src_ref=src, dst_ref=dst, send_sem=sum_send.at[i], recv_sem=sum_recv.at[i],
            device_id=target, device_id_type=MESH)

    def pair_sum(numer, crecv, s, i, n):
        copies[i].wait_recv()

        def step(tz, carry):
            f = fcol[tz, :, c]
            both = numer[tz, :, c] * f[..., 6:7] + crecv[tz].astype(F32) * f[..., 7:8]
            for h in range(2):
                s[tz, :, :, h, :, 0:n] = both[:, :, 4 * h : 4 * h + 4].astype(BF16)
                if i == 1:
                    s[tz, :, :, h, :, n : n + AUX] = f[:, :, 4 * h : 4 * h + 4].astype(BF16)
            return carry

        lax.fori_loop(0, 4, step, 0)

    def give(s, r, i, steps):
        def step(to, number, device):
            sum_copy(s.at[to], r.at[number], i - 1, device).start()

        every_chip(step, steps)
        if 0 in steps:
            pltpu.make_async_copy(s.at[z, yh, x, yl], r.at[0], sum_recv.at[i - 1]).start()

    numer_part(512, 256, numer_b, 0)
    pl.semaphore_wait(in_sem.at[1], 3)
    pair_sum(numer_a, crecv_a, sa, 1, COLS[0])
    give(sa, ra, 1, (2,))
    numer_part(768, 256, numer_b, 256)
    give(sa, ra, 1, (1,))
    numer_part(1024, 256, numer_b, 512)
    pair_send(numer_b, csend_b, crecv_b, 2)
    give(sa, ra, 1, (3, 0))
    pair_sum(numer_b, crecv_b, sb, 2, COLS[1])
    give(sb, rb, 2, FAR_FIRST)

    def combine_step(t, carry):
        rows = pl.ds(pl.multiple_of(t * 256, 256), 256)
        e = logit[rows]
        e = jnp.exp(e - jnp.max(e, axis=1, keepdims=True))
        comb[rows] = (e / jnp.sum(e, axis=1, keepdims=True)).astype(BF16)
        return carry

    lax.fori_loop(0, TOK // 256, combine_step, 0)
    comb_copy = pltpu.make_async_copy(comb, comb_out, out_sem.at[0])
    comb_copy.start()

    sum_copy(ra, ra, 0, partner).wait_recv()
    a = ra[:, :, COLS[0] : COLS[0] + AUX].astype(F32)
    tops = a[..., 0:1] + a[..., 1:2] + a[..., 2:3]
    tots = a[..., 3:4] + a[..., 4:5] + a[..., 5:6]
    factor = jnp.exp(tops - jnp.max(tops, axis=0, keepdims=True))
    own_total = jnp.sum(factor * tots, axis=0)
    fb[...] = jnp.broadcast_to(factor, fb.shape)
    own_total = jnp.broadcast_to(own_total, (4, 128))

    def gather_sum(r, k, to):
        cols = pl.ds(k * 128, 128)
        x8[0:4, to : to + 128] = jnp.sum(r[:, :, cols].astype(F32) * fb[...], axis=0) / own_total

    x8[4:8] = jnp.zeros((4, D), F32)
    for i, r in enumerate((ra, rb)):
        if i:
            sum_copy(r, r, i, partner).wait_recv()
        for k in range(COLS[i] // 128):
            gather_sum(r, k, START[i] + k * 128)

    gain_in.wait()
    normed = (x8[...] * gain[...]).astype(BF16)
    win_in.wait()
    wout_in.wait()
    hidden = jax.nn.gelu(jnp.dot(normed, win[...], preferred_element_type=F32)).astype(BF16)
    gs[...] = jnp.dot(hidden, wout[...], preferred_element_type=F32)[0:4].astype(BF16)

    def row_copy(src, dst, i, target):
        return pltpu.make_async_remote_copy(
            src_ref=src, dst_ref=dst, send_sem=row_send.at[i], recv_sem=row_recv.at[i],
            device_id=target, device_id_type=MESH)

    for dz in FAR_FIRST:
        def show(to, number, device, dz=dz):
            row_copy(gs, g.at[z, yh, c, x, yl], dz, device).start()

        every_chip(show, (dz,))
    pltpu.make_async_copy(gs, g.at[z, yh, c, x, yl], row_recv.at[0]).start()
    for dz in FAR_FIRST:
        slab = g.at[(z + 4 - dz) % 4, :, c]
        row_copy(slab, slab, dz, partner).wait_recv()
        copies.append(pair(slab, slab, 3 + dz))
        copies[-1].start()
    for i, dz in enumerate(FAR_FIRST):
        tz = (z + 4 - dz) % 4
        copies[3 + i].wait_recv()
        gf[tz] = g[tz].reshape(128, D)

    for copy in copies:
        copy.wait_send()
    for i, r in enumerate((ra, rb)):
        sent = r.at[pl.ds(0, 63)]
        sum_copy(sent, sent, i, partner).wait_send()
    slab = g.at[0, :, 0]
    for dz in (1, 2, 3):
        row_copy(slab, slab, dz, partner).wait_send()
    part = ra.at[pl.ds(0, 30)]
    row_copy(part, part, 0, partner).wait_send()
    comb_copy.wait()


def mix_kernel(comb, rows, out, held, sem):
    copies = []
    for k, (at, n) in enumerate(((0, TOK), (0, TOK), (0, TOK), (0, TOK), (0, TOK // 2), (TOK // 2, TOK // 2))):
        block = (pl.ds(at, n), pl.ds(min(k, 4) * 256, 256))
        held[block] = jnp.dot(comb[block[0]], rows[:, block[1]], preferred_element_type=F32).astype(BF16)
        copies.append(pltpu.make_async_copy(held.at[block], out.at[block], sem.at[k]))
        copies[k].start()
    for copy in copies:
        copy.wait()


def on_device(tokens, slot_keys, norm_gain, w_in, w_out):
    anywhere = pl.BlockSpec(memory_space=pl.ANY)

    def stay(v):
        return pltpu.with_memory_space_constraint(v, pltpu.HBM)

    held = pl.BlockSpec(memory_space=pltpu.VMEM)
    vmem = pltpu.VMEM
    sem = pltpu.SemaphoreType.DMA
    gathered, combine = pl.pallas_call(
        kernel,
        out_shape=(
            jax.ShapeDtypeStruct((4, 128, D), BF16),
            jax.ShapeDtypeStruct((TOK, SLOTS), BF16),
        ),
        in_specs=[anywhere] * 5,
        out_specs=(held, anywhere),
        scratch_shapes=[
            vmem((TOK, D), BF16),
            vmem((D, SLOTS), BF16),
            vmem((TOK, SLOTS), F32),
            vmem((SLOTS, TOK), BF16),
            vmem((TOK, SLOTS), BF16),
            *(vmem((4, 2, 2, 4, 8, n), F32) for n in COLS),
            vmem((1, D), F32),
            vmem((D, FF), BF16),
            vmem((FF, D), BF16),
            vmem((2, 8, SLOTS), F32),
            vmem((4, 2, 2, 4, 8, AUX), F32),
            vmem((64, 4, 128), F32),
            *(vmem((4, 2, 4, 8, n), BF16) for n in COLS),
            *(vmem((4, 2, 4, 8, n), BF16) for n in COLS),
            *(vmem((4, 2, 4, 2, 4, n), BF16) for n in (COLS[0] + AUX, COLS[1])),
            *(vmem((64, 4, n), BF16) for n in (COLS[0] + AUX, COLS[1])),
            vmem((8, D), F32),
            vmem((4, D), BF16),
            vmem((4, 2, 2, 4, 2, 4, D), BF16),
            pltpu.SemaphoreType.REGULAR((2,)),
            sem((8,)),
            sem((1,)),
            sem((7,)),
            sem((7,)),
            sem((2,)),
            sem((2,)),
            sem((4,)),
            sem((4,)),
        ],
        compiler_params=pltpu.CompilerParams(
            collective_id=0, has_side_effects=True, vmem_limit_bytes=48 << 20
        ),
        name="route",
    )(*(stay(v) for v in (tokens, slot_keys, norm_gain, w_in, w_out)))
    return pl.pallas_call(
        mix_kernel,
        out_shape=jax.ShapeDtypeStruct((TOK, D), BF16),
        in_specs=[held, held],
        out_specs=anywhere,
        scratch_shapes=[vmem((TOK, D), BF16), sem((6,))],
        compiler_params=pltpu.CompilerParams(vmem_limit_bytes=12 << 20),
        name="mix",
    )(combine, gathered.reshape(SLOTS, D))


def solution(mesh):
    return jax.shard_map(
        on_device,
        mesh=mesh,
        in_specs=(
            P(("seq", "grp"), None),
            P(),
            P(("seq", "grp"), None),
            P(("seq", "grp"), None, None),
            P(("seq", "grp"), None, None),
        ),
        out_specs=P(("seq", "grp"), None),
        check_vma=False,
    )
```
